32 devices in a mesh: expert: 16 (over z, y, core), tensor: 2 (over x).
Axes of the slice: x: 2, y: 2, z: 4, core: 2. Of those that a mesh axis runs over, the one named last changes fastest.
Arguments:
- tokens: bfloat16 [18912, 768], P('expert'), may hold values from -6 to 6
- teacher: bfloat16 [18912, 768], P('expert'), may hold values from -12 to 12
- valid_flags: int32 [96], P('expert'), may hold values from 0 to 1, as said below
- routes: int32 [18912, 2], P('expert'), may hold values from 0 to 7, all different within a row; in each aligned block of 1182 rows (0 to 1181, 1182 to 2363, ...) at most 440 rows name the same one
- capacity: int32 [8], replicated, may hold values from 220 to 440, as said below
- norm_gains: bfloat16 [4, 768], replicated, may hold values from 0.5 to 1.5
- norm_biases: bfloat16 [4, 768], replicated, may hold values from -0.59765625 to 0.59765625
- attn_qkv: bfloat16 [2, 3, 768, 768], P(None, None, None, 'tensor'), may hold values from -0.21875 to 0.21875
- attn_out: bfloat16 [2, 768, 768], P(None, 'tensor'), may hold values from -1.75 to 1.75
- mlp_in: bfloat16 [768, 3072], P(None, 'tensor'), may hold values from -0.21875 to 0.21875
- mlp_out: bfloat16 [3072, 768], P('tensor'), may hold values from -0.109375 to 0.109375
- router: bfloat16 [768, 8], replicated, may hold values from -0.15625 to 0.15625
- expert_in: bfloat16 [16, 768, 1536], P('expert', None, 'tensor'), may hold values from -0.21875 to 0.21875
- expert_out: bfloat16 [16, 1536, 768], P('expert', 'tensor'), may hold values from -0.109375 to 0.109375
Outputs:
- activations: bfloat16 [18912, 768], P('expert')
- input_grad: bfloat16 [18912, 768], P('expert')
- gain_grad: float32 [4, 768], P(None, 'expert')
- bias_grad: float32 [3, 768], P(None, 'expert')
- expert_norm_bias_grad: float32 [768], P('expert')
- qkv_grad: float32 [2, 3, 768, 768], P(None, None, 'expert', 'tensor')
- out_proj_grad: float32 [2, 768, 768], P(None, 'tensor', 'expert')
- mlp_in_grad: float32 [768, 3072], P('expert', 'tensor')
- mlp_out_grad: float32 [3072, 768], P('tensor', 'expert')
- router_grad: float32 [768, 8], P('expert')
- expert_in_grad: float32 [16, 768, 1536], P('expert', None, 'tensor')
- expert_out_grad: float32 [16, 1536, 768], P('expert', 'tensor')
The draws below stay inside these ranges and needn't reach their ends.
Inputs may be any that keep to these rules, and one draw needn't show every extreme that they name: `valid_flags`: 1 marks an image whose tokens count in the loss; image 0 is always valid. `routes`: the two experts of a token differ; among the rows of one index of expert no expert is named by more than 440 rows, and exactly 440 in some. `capacity`: exactly 440 for at least one expert.
All inputs are finite; a program needn't handle non-finite values.
Results may differ from the reference program's by a relative error of at most 0.035.
Values may be sent and summed in bfloat16 or wider, within the bound.
No kernel may reach another device: no remote copies, remote signals or barrier semaphores. Data moves between devices by JAX's collectives and lax.ppermute only.
A program may use at most 256 MiB of HBM per device.

```python
import math
import jax
import jax.numpy as jnp
import numpy as np
from jax import lax

D = 768
HD = 64
FF = 3072
SEQ = 197
IMG_DEV = 6
TOK_DEV = 1182
IMAGES = 96
TOKENS = 18912
EXPERTS = 8
CAP = 440
N_EXPERT = 16
N_TENSOR = 2


def draw_valid_flags(key, part):
    positions = jnp.arange(IMAGES, dtype=jnp.int32)
    drawn_ints = jax.random.randint(key, (IMAGES,), 0, 4 * IMAGES, dtype=jnp.int32)
    return ((drawn_ints < IMAGES + 3 * positions) | (positions == 0)).astype(jnp.int32)


def draw_capacity(key, part):
    key_base = jax.random.fold_in(key, 11)
    key_pick = jax.random.fold_in(key, 23)
    base_caps = jax.random.randint(key_base, (EXPERTS,), CAP // 2, CAP + 1, dtype=jnp.int32)
    chosen = jax.random.randint(key_pick, (), 0, EXPERTS, dtype=jnp.int32)
    return jnp.where(jnp.arange(EXPERTS, dtype=jnp.int32) == chosen, CAP, base_caps).astype(jnp.int32)


def level_of(key, extent, cuts, smallest, largest):
    def one(axis_at, parts):
        heights = jax.random.uniform(jax.random.fold_in(jax.random.fold_in(key, 6), axis_at), (parts,), jnp.float32, smallest / len(cuts), largest / len(cuts))
        return jnp.repeat(jnp.exp(heights), extent[axis_at] // parts).reshape((-1,) + (1,) * (len(extent) - axis_at - 1))

    loudness = one(*cuts[0])
    for cut in cuts[1:]:
        loudness = loudness * one(*cut)
    return loudness


def assign_block(own_key, own, number, rows, number_of, top, reach, lean):
    sequence = jax.random.permutation(own_key, number_of)
    crowded, usual = shares(number_of, rows * top, reach, lean, True), shares(number_of, rows * top, reach, lean, False)
    places = jnp.arange(number_of)

    def named(lengths, offset_by):
        used = int((lengths > 0).sum())
        fixed = max(1, used // 4)
        shifted = fixed + (places - fixed + offset_by * (used - fixed)) % max(1, number_of - fixed)
        return jnp.zeros((number_of,), jnp.int32).at[sequence[jnp.where(places < fixed, places, shifted)]].set(jnp.asarray(lengths, jnp.int32))

    lengths = jnp.where(number % 4 == 0, named(crowded, number // 4), named(usual, number - number // 4 - 1))
    mixed = jax.random.permutation(jax.random.fold_in(own, 3), number_of)
    source_of, taker = mixed[0:number_of // 2 * 2:2], mixed[1:number_of // 2 * 2:2]
    slack = jnp.minimum(lengths[source_of] - 1, reach - lengths[taker]) // 2
    slack = jnp.where((source_of == sequence[0]) | (taker == sequence[0]) | (lengths[taker] == 0), 0, jnp.maximum(slack, 0))
    shifted = jax.random.randint(jax.random.fold_in(own, 4), (number_of // 2,), 0, 1 << 20) % (slack + 1)
    lengths = lengths.at[source_of].add(-shifted).at[taker].add(shifted)
    items = jnp.searchsorted(jnp.cumsum(lengths), jnp.arange(rows * top), side="right").astype(jnp.int32)
    table = items.reshape(top, rows).T
    table = table[jax.random.permutation(jax.random.fold_in(own, 1), rows)]
    offset_by = jax.random.randint(jax.random.fold_in(own, 2), (rows, 1), 0, top)
    return jnp.take_along_axis(table, (jnp.arange(top)[None, :] + offset_by) % top, axis=1)


def shares(number_of, total, bound, lean, full):
    loads = [(1 << 20) // math.isqrt(rank ** lean) + 1 for rank in range(1, number_of + 1)]
    largest = bound if full else min(bound, max(-(-total // number_of), total * loads[0] // sum(loads)))
    least = 1 if total - largest >= number_of - 1 else 0
    holding, spare = [largest] + [least] * (number_of - 1), total - largest - least * (number_of - 1)
    while spare > 0:
        free = [i for i in range(1, number_of) if holding[i] < largest] or [i for i in range(1, number_of) if holding[i] < bound]
        mass, budget = sum([loads[i] for i in free]), spare
        for i in free:
            addition = min(bound - holding[i], max(1, budget * loads[i] // mass), spare)
            holding[i] = holding[i] + addition
            spare = spare - addition
    return np.array(holding)


def gaussian(rng, dims, scale, bound, split=(), kind=jnp.bfloat16):
    array = jax.random.normal(rng, dims, jnp.float32) * scale
    if len(split) > 0:
        array = level_of(rng, dims, split, -0.22, 0.18) * array
    return jnp.clip(array, min=-bound, max=bound).astype(kind)


def setup_inputs(seed: int = 0) -> dict:
    key_list = jax.random.split(jax.random.key(seed), 15)
    tokens = gaussian(key_list[0], (TOKENS, D), 1.0, 6.0, ((0, 16),))
    teacher = gaussian(key_list[1], (TOKENS, D), 2.0, 12.0, ((0, 16),))
    valid_flags = draw_valid_flags(jax.random.fold_in(key_list[14], 71), 0)
    routes_keys = jax.random.split(jax.random.fold_in(key_list[3], 1), TOKENS // TOK_DEV)
    routes_turns = jax.random.permutation(jax.random.fold_in(key_list[3], 3), TOKENS // TOK_DEV)
    routes = jax.vmap(lambda own, number: assign_block(jax.random.fold_in(key_list[3], 2), own, number, TOK_DEV, EXPERTS, 2, CAP, 2))(routes_keys, routes_turns).reshape((TOKENS, 2))
    capacity = draw_capacity(jax.random.fold_in(key_list[14], 71), 0)
    norm_gains = jnp.clip(1.0 + 0.1 * jax.random.normal(key_list[5], (4, D), jnp.float32), 0.5, 1.5).astype(jnp.bfloat16)
    norm_biases = gaussian(key_list[6], (4, D), 0.1, 0.59765625)
    attn_qkv = gaussian(key_list[7], (2, 3, D, D), D ** -0.5, 0.21875, ((3, 2),))
    attn_out = gaussian(key_list[8], (2, D, D), (D // 64) ** -0.5, 1.75, ((1, 2),))
    mlp_in = gaussian(key_list[9], (D, FF), D ** -0.5, 0.21875, ((1, 2),))
    mlp_out = gaussian(key_list[10], (FF, D), FF ** -0.5, 0.109375, ((0, 2),))
    router = gaussian(key_list[11], (D, EXPERTS), (2 * D) ** -0.5, 0.15625)
    expert_in = gaussian(key_list[12], (2 * EXPERTS, D, FF // 2), D ** -0.5, 0.21875, ((0, 16), (2, 2)))
    expert_out = gaussian(key_list[13], (2 * EXPERTS, FF // 2, D), FF ** -0.5, 0.109375, ((0, 16), (1, 2)))
    return {"tokens": tokens, "teacher": teacher, "valid_flags": valid_flags, "routes": routes, "capacity": capacity, "norm_gains": norm_gains, "norm_biases": norm_biases, "attn_qkv": attn_qkv, "attn_out": attn_out, "mlp_in": mlp_in, "mlp_out": mlp_out, "router": router, "expert_in": expert_in, "expert_out": expert_out}


@jax.custom_vjp
def low(v):
    return lax.optimization_barrier(v.astype(jnp.bfloat16)).astype(jnp.float32)

@jax.custom_vjp
def low_back(v):
    return v

def low_keep(v):
    return (low(v), None)

def low_pass(kept, grad):
    return (grad,)

def back_keep(v):
    return (v, None)

def back_low(kept, grad):
    return (low(grad),)
low.defvjp(low_keep, low_pass)
low_back.defvjp(back_keep, back_low)
HIGHEST = lax.Precision.HIGHEST
epsilon = 1e-06

def normalize(values, gain_row, bias_row):
    center = values - lax.optimization_barrier(jnp.mean(values, axis=-1, keepdims=True))
    scaled = center * lax.rsqrt(lax.optimization_barrier(jnp.mean(center * center, axis=-1, keepdims=True)) + epsilon)
    return scaled * gain_row + bias_row

def attention_rows(row_block, gain_row, bias_row, qkv_weight, out_weight):
    normed = low(normalize(row_block, gain_row, bias_row))
    group_width = D // N_TENSOR
    summed = jnp.zeros_like(row_block)
    for group_index in range(N_TENSOR):
        first_col = group_index * group_width
        shared = low_back(normed)
        packed = jnp.einsum('td,sdc->stc', shared, qkv_weight[:, :, first_col:first_col + group_width], precision=HIGHEST)
        packed = low(low_back(packed)).reshape(3, IMG_DEV, SEQ, group_width // HD, HD)
        scores = jnp.einsum('bqhe,bkhe->bhqk', packed[0], packed[1], precision=HIGHEST) * HD ** (-0.5)
        attn_probs = low(jax.nn.softmax(low_back(scores), axis=-1))
        mixed_rows = jnp.einsum('bhqk,bkhe->bqhe', attn_probs, packed[2], precision=HIGHEST).reshape(TOK_DEV, group_width)
        mixed_rows = low(low_back(mixed_rows))
        branch = jnp.dot(mixed_rows, out_weight[first_col:first_col + group_width], precision=HIGHEST)
        summed = summed + low(low_back(branch))
    return row_block + summed

def attention_layer(residual, gain_row, bias_row, qkv_weight, out_weight):
    blocks = residual.reshape(N_EXPERT, TOK_DEV, D)
    step_rows = jax.checkpoint(lambda row_block: attention_rows(row_block, gain_row, bias_row, qkv_weight, out_weight))
    return lax.map(step_rows, blocks).reshape(TOKENS, D)

def dense_layer(residual, gain_row, bias_row, weight_in, weight_out):
    normed = low(normalize(residual, gain_row, bias_row))
    group_width = FF // N_TENSOR
    summed = jnp.zeros_like(residual)
    for group_index in range(N_TENSOR):
        first_col = group_index * group_width
        shared = low_back(normed)
        hidden = low_back(jnp.dot(shared, weight_in[:, first_col:first_col + group_width], precision=HIGHEST))
        active = low(jax.nn.gelu(hidden, approximate=True))
        branch = jnp.dot(active, weight_out[first_col:first_col + group_width], precision=HIGHEST)
        summed = summed + low(low_back(branch))
    return residual + summed

def expert_one(operands):
    rows_in, halves_in, halves_out = operands
    group_width = FF // (2 * N_TENSOR)
    total_rows = jnp.zeros_like(rows_in)
    for half_index in range(2):
        shared = low_back(rows_in)
        part_sum = jnp.zeros_like(rows_in)
        for group_index in range(N_TENSOR):
            first_col = group_index * group_width
            group_rows = low_back(shared)
            hidden = low_back(jnp.dot(group_rows, halves_in[half_index][:, first_col:first_col + group_width], precision=HIGHEST))
            active = low(jax.nn.gelu(hidden, approximate=True))
            part_sum = part_sum + low(jnp.dot(active, halves_out[half_index][first_col:first_col + group_width], precision=HIGHEST))
        total_rows = total_rows + low(low_back(part_sum))
    return total_rows

def place_pairs(block_routes, capacity):
    expert_of = jnp.concatenate([block_routes[:, 0], block_routes[:, 1]]).astype(jnp.int32)
    onehot = (expert_of[:, None] == jnp.arange(EXPERTS, dtype=jnp.int32)[None, :]).astype(jnp.int32)
    earlier = (jnp.cumsum(onehot, axis=0) - onehot).astype(jnp.int32)
    position = lax.optimization_barrier(jnp.sum(earlier * onehot, axis=1)).astype(jnp.int32)
    limit_of = lax.optimization_barrier(jnp.sum(onehot * capacity[None, :], axis=1)).astype(jnp.int32)
    return ((expert_of * CAP + position).astype(jnp.int32), position < limit_of)

def expert_layer(residual, gain_row, bias_row, router_weight, weight_in, weight_out, routes, slot_of, kept_mask):
    normed = low(normalize(residual, gain_row, bias_row))
    logits = low_back(jnp.dot(normed, router_weight, precision=HIGHEST))
    chosen = jnp.take_along_axis(logits, routes, axis=1)
    gate_vals = jax.nn.softmax(chosen, axis=1)
    target = jnp.where(kept_mask, slot_of, EXPERTS * CAP).astype(jnp.int32)
    fetch_at = jnp.where(kept_mask, slot_of, 0).astype(jnp.int32)
    gate_pairs = gate_vals.reshape(N_EXPERT, TOK_DEV, 2).transpose(0, 2, 1)[..., None]
    mask_pairs = kept_mask.reshape(N_EXPERT, 2, TOK_DEV, 1)
    shared = normed.reshape(N_EXPERT, TOK_DEV, D)
    pair_rows = jnp.concatenate([shared, shared], axis=1)
    filled = jax.vmap(lambda rows_one, where_to: jnp.zeros((EXPERTS * CAP, D), jnp.float32).at[where_to].set(rows_one, mode='drop'))(pair_rows, target)
    by_expert = filled.reshape(N_EXPERT, EXPERTS, CAP, D).transpose(1, 0, 2, 3).reshape(EXPERTS, N_EXPERT * CAP, D)
    halves_in = weight_in.reshape(EXPERTS, 2, D, FF // 2)
    halves_out = weight_out.reshape(EXPERTS, 2, FF // 2, D)
    outputs = lax.map(jax.checkpoint(expert_one), (by_expert, halves_in, halves_out))
    by_source = outputs.reshape(EXPERTS, N_EXPERT, CAP, D).transpose(1, 0, 2, 3).reshape(N_EXPERT, EXPERTS * CAP, D)
    picked = jax.vmap(lambda source_rows, index_rows: source_rows[index_rows])(by_source, fetch_at)
    picked = jnp.where(mask_pairs, picked.reshape(N_EXPERT, 2, TOK_DEV, D), 0.0)
    return residual + lax.optimization_barrier(jnp.sum(gate_pairs * picked, axis=1)).reshape(TOKENS, D)

def reference(tokens, teacher, valid_flags, routes, capacity, norm_gains, norm_biases, attn_qkv, attn_out, mlp_in, mlp_out, router, expert_in, expert_out):
    slot_of, kept_mask = jax.vmap(place_pairs, in_axes=(0, None))(routes.reshape(N_EXPERT, TOK_DEV, 2), capacity)
    valid_rows = jnp.repeat(valid_flags.astype(jnp.float32), SEQ)[:, None]
    valid_count = SEQ * jnp.sum(valid_flags.astype(jnp.float32))
    target_rows = teacher.astype(jnp.float32)

    def forward(residual, gain_rows, biases, qkv_weight, out_weight, dense_in, dense_out, router_weight, expert_w_in, expert_w_out):
        residual = attention_layer(residual, gain_rows[0], biases[0], qkv_weight[0], out_weight[0])
        residual = dense_layer(residual, gain_rows[1], biases[1], dense_in, dense_out)
        residual = attention_layer(residual, gain_rows[2], biases[2], qkv_weight[1], out_weight[1])
        residual = expert_layer(residual, gain_rows[3], biases[3], router_weight, expert_w_in, expert_w_out, routes, slot_of, kept_mask)
        differ = residual - target_rows
        return (TOKENS / (2.0 * valid_count) * jnp.sum(valid_rows * differ * differ), residual)
    inputs = tuple((argument.astype(jnp.float32) for argument in (tokens, norm_gains, norm_biases, attn_qkv, attn_out, mlp_in, mlp_out, router, expert_in, expert_out)))
    loss_value, pull_back, final_rows = jax.vjp(forward, *inputs, has_aux=True)
    gradients = pull_back(jnp.ones_like(loss_value))
    return (final_rows.astype(jnp.bfloat16), gradients[0].astype(jnp.bfloat16), gradients[1], gradients[2][:3], gradients[2][3], gradients[3], gradients[4], gradients[5], gradients[6], gradients[7], gradients[8], gradients[9])
```

```python
import jax
import jax.numpy as jnp
from jax import lax
from jax.sharding import PartitionSpec as P

HD = 64
SEQ = 197
ROWS = 208
EPS = 1e-06
BF = jnp.bfloat16
F32 = jnp.float32


def mm(a, b, dims):
    return lax.dot_general(a, b, (dims, ((), ())), preferred_element_type=F32)


NN = ((1,), (0,))
NT = ((1,), (1,))
TN = ((0,), (0,))


def swap(value, axis, distance):
    size = lax.axis_size(axis)
    return lax.ppermute(value, axis, [(k, k ^ distance) for k in range(size)])


def normalize(values, gain_row, bias_row):
    center = values - jnp.mean(values, axis=-1, keepdims=True)
    scaled = center * lax.rsqrt(jnp.mean(center * center, axis=-1, keepdims=True) + EPS)
    return scaled * gain_row + bias_row


def norm_backward(values, gain_row, bias_row, grad_normed):
    pull_back = jax.vjp(normalize, values, gain_row, bias_row)[1]
    return pull_back(grad_normed)


def gelu_both(x):
    k = 0.7978845608028654
    a = 0.044715
    th = jnp.tanh(k * (x + a * x * x * x))
    half = 0.5 * (1.0 + th)
    return x * half, half + 0.5 * x * (1.0 - th * th) * k * (1.0 + 3.0 * a * x * x)


def heads_of(rows, images):
    return rows.reshape(images, ROWS, -1, HD)


def attend_forward(normed, qkv, out, images):
    packed = [mm(normed, w, NN).astype(BF) for w in qkv]
    q, k, v = (heads_of(p, images) for p in packed)
    scores = jnp.einsum("bqhe,bkhe->bhqk", q, k, preferred_element_type=F32) * HD ** (-0.5)
    keys = lax.broadcasted_iota(jnp.int32, scores.shape, 3)
    scores = jnp.where(keys < SEQ, scores, -1e30)
    total = jax.nn.logsumexp(scores, axis=-1, keepdims=True)
    probs = jnp.exp(scores - total).astype(BF)
    mixed = jnp.einsum("bhqk,bkhe->bqhe", probs, v, preferred_element_type=F32)
    mixed = mixed.reshape(normed.shape[0], -1).astype(BF)
    return mm(mixed, out, NN), (packed, total, mixed)


def attend_backward(grad_low, out, qkv, kept, images):
    packed, total, mixed = kept
    q, k, v = (heads_of(p, images) for p in packed)
    grad_mixed = heads_of(mm(grad_low, out, NT).astype(BF), images)
    scores = jnp.einsum("bqhe,bkhe->bhqk", q, k, preferred_element_type=F32) * HD ** (-0.5)
    keys = lax.broadcasted_iota(jnp.int32, scores.shape, 3)
    probs = jnp.where(keys < SEQ, jnp.exp(scores - total), 0.0)
    grad_probs = jnp.einsum("bqhe,bkhe->bhqk", grad_mixed, v, preferred_element_type=F32)
    inner = jnp.sum(grad_probs * probs, axis=-1, keepdims=True)
    grad_scores = (probs * (grad_probs - inner)).astype(BF)
    scale = HD ** (-0.5)
    gq = jnp.einsum("bhqk,bkhe->bqhe", grad_scores, k, preferred_element_type=F32) * scale
    gk = jnp.einsum("bhqk,bqhe->bkhe", grad_scores, q, preferred_element_type=F32) * scale
    gv = jnp.einsum("bhqk,bqhe->bkhe", probs.astype(BF), grad_mixed, preferred_element_type=F32)
    grads = [g.reshape(grad_low.shape[0], -1).astype(BF) for g in (gq, gk, gv)]
    grad_normed = sum(mm(g, w, NT) for g, w in zip(grads, qkv))
    return grad_normed, grads


def body(
    tokens,
    teacher,
    valid_flags,
    routes,
    capacity,
    norm_gains,
    norm_biases,
    attn_qkv,
    attn_out,
    mlp_in,
    mlp_out,
    router,
    expert_in,
    expert_out,
):
    owners = lax.axis_size("expert")
    groups = lax.axis_size("tensor")
    place = lax.axis_index("expert")
    group = lax.axis_index("tensor")
    core = place % 2
    local_rows, width = tokens.shape
    experts = router.shape[1]
    image_count = local_rows // SEQ
    images = -(-image_count // groups)
    own_rows = images * ROWS
    all_rows = groups * own_rows
    capacity_most = 4 * (3 * local_rows // (4 * experts))
    part = -(-capacity_most // (2 * groups))
    part = -(-part // 16) * 16
    slots = owners * part
    gains = norm_gains.astype(F32)
    biases = norm_biases.astype(F32)

    def relative(rows, fill, count):
        shape = rows.shape[1:]
        grid = rows.reshape((image_count, SEQ) + shape)
        grid = jnp.pad(
            grid,
            [(0, groups * images - image_count), (0, ROWS - SEQ)] + [(0, 0)] * len(shape),
            constant_values=fill,
        )
        taken = [
            lax.dynamic_slice_in_dim(grid, (group ^ d) * images, images, 0) for d in range(count)
        ]
        return jnp.concatenate(taken, 0).reshape((count * own_rows,) + shape)

    def absolute(rows):
        shape = rows.shape[1:]
        grid = rows.reshape((groups * images, ROWS) + shape)
        taken = [
            lax.dynamic_slice_in_dim(grid, (group ^ d) * images, images, 0) for d in range(groups)
        ]
        grid = jnp.concatenate(taken, 0)[:image_count, :SEQ]
        return grid.reshape((local_rows,) + shape)

    count = jnp.full((8, 128), SEQ * jnp.sum(valid_flags.astype(F32)), F32)
    step = 1
    while step < owners:
        count = count + swap(count, "expert", step)
        step *= 2
    valid_count = count[0, 0]

    order = [None]

    def chained(value):
        if order[0] is not None:
            value, _ = lax.optimization_barrier((value, order[0]))
        return value

    def gather_dense(weight):
        rows = weight.shape[0] // 2
        mine = lax.dynamic_slice_in_dim(weight, core * rows, rows, 0)
        out = [weight]
        for d in range(1, groups):
            first = swap(chained(mine), "tensor", d)
            order[0] = first
            other = swap(first, "expert", 1)
            low = jnp.where(core == 0, first, other)
            high = jnp.where(core == 0, other, first)
            out.append(jnp.concatenate([low, high], 0))
        return out

    def gather_expert(weight):
        out = [weight]
        for d in range(1, groups):
            first = swap(chained(weight), "tensor", d)
            order[0] = first
            out.append(first)
        return out + [swap(w, "expert", 1) for w in out]

    def gather_qkv(weight):
        parts = gather_dense(weight.reshape(3 * width, -1))
        parts = [p.reshape(3, width, -1) for p in parts]
        return [jnp.concatenate([p[s] for p in parts], 1) for s in range(3)]

    qkv_first = gather_qkv(attn_qkv[0])
    out_first = jnp.concatenate(gather_dense(attn_out[0]), 0)
    dense_in = gather_dense(mlp_in)
    dense_out = gather_dense(mlp_out)
    qkv_second = gather_qkv(attn_qkv[1])
    out_second = jnp.concatenate(gather_dense(attn_out[1]), 0)
    whole_in = gather_expert(expert_in[0])
    whole_out = gather_expert(expert_out[0])

    expert_of = jnp.concatenate([routes[:, 0], routes[:, 1]])
    onehot = (expert_of[:, None] == jnp.arange(experts, dtype=jnp.int32)[None, :]).astype(jnp.int32)
    earlier = jnp.cumsum(onehot, axis=0) - onehot
    position = jnp.sum(earlier * onehot, axis=1)
    kept_mask = position < jnp.sum(onehot * capacity[None, :], axis=1)
    quarter = position // part
    row_of = (2 * expert_of + quarter % 2) * part + position % part
    row_of = jnp.where(kept_mask & (quarter // 2 == group), row_of, -1)
    row_of = relative(row_of.reshape(2, local_rows).T, -1, groups)
    routes_rel = relative(routes, 0, groups)
    valid_rows = relative(jnp.repeat(valid_flags.astype(F32), SEQ)[:, None], 0, groups)

    start = relative(tokens, 0, 1).astype(F32)
    normed_first = normalize(start, gains[0], biases[0]).astype(BF)
    branch, saved_first = attend_forward(normed_first, qkv_first, out_first, images)
    after_attn = start + branch
    normed_dense = normalize(after_attn, gains[1], biases[1]).astype(BF)
    dense_pairs = [gelu_both(mm(normed_dense, w, NN)) for w in dense_in]
    dense_act = [a.astype(BF) for a, _ in dense_pairs]
    dense_slope = [b.astype(BF) for _, b in dense_pairs]
    after_dense = after_attn + sum(mm(a, w, NN) for a, w in zip(dense_act, dense_out))
    normed_second = normalize(after_dense, gains[2], biases[2]).astype(BF)
    branch, saved_second = attend_forward(normed_second, qkv_second, out_second, images)
    after_second = after_dense + branch
    normed_expert = normalize(after_second, gains[3], biases[3]).astype(BF)
    normed_all = jnp.concatenate(
        [normed_expert] + [swap(normed_expert, "tensor", d) for d in range(1, groups)], 0
    )

    logits = mm(normed_all, router, NN)
    picker = routes_rel[:, :, None] == jnp.arange(experts, dtype=jnp.int32)[None, None, :]
    chosen = jnp.sum(jnp.where(picker, logits[:, None, :], 0.0), axis=2)
    gate_vals = jax.nn.softmax(chosen, axis=1)

    slot_ids = jnp.arange(slots, dtype=jnp.int32)
    take_first = slot_ids[:, None] == row_of[None, :, 0]
    take_second = slot_ids[:, None] == row_of[None, :, 1]
    take = (take_first | take_second).astype(BF)

    def across(rows):
        return lax.all_to_all(
            rows.reshape(owners, part, width), "expert", split_axis=0, concat_axis=0, tiled=True
        ).reshape(slots, width)

    rows_in = across(mm(take, normed_all, NN).astype(BF))
    pairs = [gelu_both(mm(rows_in, w, NN)) for w in whole_in]
    act = [a.astype(BF) for a, _ in pairs]
    slope = [b.astype(BF) for _, b in pairs]
    merged = across(sum(mm(a, w, NN) for a, w in zip(act, whole_out)).astype(BF))

    weights = jnp.where(take_first, gate_vals[None, :, 0], 0.0) + jnp.where(
        take_second, gate_vals[None, :, 1], 0.0
    )
    weights = weights.astype(BF)
    combined = mm(weights, merged, TN)
    final = after_second + combined[:own_rows]
    for d in range(1, groups):
        sent = combined[d * own_rows : (d + 1) * own_rows].astype(BF)
        final = final + swap(sent, "tensor", d).astype(F32)
    final_low = final.astype(BF)
    final_all = jnp.concatenate(
        [final_low] + [swap(final_low, "tensor", d) for d in range(1, groups)], 0
    )
    activations = absolute(final_all)
    teacher_rel = relative(teacher, 0, groups).astype(F32)
    scale = (local_rows * owners / valid_count) * valid_rows
    grad_final = scale[:own_rows] * (final - teacher_rel[:own_rows])
    grad_all = scale * (final_all.astype(F32) - teacher_rel)
    grad_all = jnp.concatenate([grad_final, grad_all[own_rows:]], 0).astype(BF)

    taken = mm(take, grad_all, NN)
    gate_of_slot = jnp.sum(
        jnp.where(take_first, gate_vals[None, :, 0], 0.0)
        + jnp.where(take_second, gate_vals[None, :, 1], 0.0),
        axis=1,
        keepdims=True,
    )
    grad_slot_gate = jnp.sum(taken * merged.astype(F32), axis=1, keepdims=True)
    grad_out_rows = across((gate_of_slot * taken).astype(BF))
    grad_gates = jnp.stack(
        [
            jnp.sum(jnp.where(take_first, grad_slot_gate, 0.0), axis=0),
            jnp.sum(jnp.where(take_second, grad_slot_gate, 0.0), axis=0),
        ],
        0,
    )
    grad_own = grad_gates[:, :own_rows]
    for d in range(1, groups):
        grad_own = grad_own + swap(
            grad_gates[:, d * own_rows : (d + 1) * own_rows], "tensor", d
        )
    grad_own = grad_own.T
    grad_hidden = [
        (mm(grad_out_rows, w, NT) * s.astype(F32)).astype(BF) for w, s in zip(whole_out, slope)
    ]
    grad_rows = sum(mm(g, w, NT) for g, w in zip(grad_hidden, whole_in)).astype(BF)
    grad_back = across(grad_rows)

    def share_expert(parts):
        kept = []
        for d in range(groups):
            got = swap(parts[groups + d].astype(BF), "expert", 1)
            kept.append(parts[d] + got.astype(F32))
        total = kept[0]
        for d in range(1, groups):
            total = total + swap(kept[d].astype(BF), "tensor", d).astype(F32)
        return total

    grad_expert_out = share_expert([mm(a, grad_out_rows, TN) for a in act])
    grad_expert_in = share_expert([mm(rows_in, g, TN) for g in grad_hidden])

    own_gates = gate_vals[:own_rows]
    grad_chosen = own_gates * (grad_own - jnp.sum(own_gates * grad_own, axis=1, keepdims=True))
    grad_logits = jnp.sum(
        jnp.where(picker[:own_rows], grad_chosen[:, :, None], 0.0), axis=1
    ).astype(BF)
    grad_router = mm(grad_logits, normed_expert, TN)
    returned = mm(take, grad_back, TN)
    grad_normed = returned[:own_rows] + mm(grad_logits, router, NT)
    for d in range(1, groups):
        sent = returned[d * own_rows : (d + 1) * own_rows].astype(BF)
        grad_normed = grad_normed + swap(sent, "tensor", d).astype(F32)
    back, gain_four, bias_four = norm_backward(after_second, gains[3], biases[3], grad_normed)
    grad_second = grad_final + back

    block = width // owners
    feature = jnp.arange(width, dtype=jnp.int32)
    ahead, turned, step = feature // block, 0, 1
    while step < owners:
        turned = turned * 2 + ahead % 2
        ahead = ahead // 2
        step *= 2
    source = (turned ^ place) * block + feature % block
    mover = (feature[:, None] == source[None, :]).astype(BF)

    def moved(rows):
        return mm(rows, mover, NN).astype(BF)

    def share_dense(parts):
        rows = width // 2
        kept = []
        for d in range(groups):
            got = swap(parts[d][rows:].astype(BF), "expert", 1)
            kept.append(parts[d][:rows] + got.astype(F32))
        total = kept[0]
        for d in range(1, groups):
            total = total + swap(kept[d].astype(BF), "tensor", d).astype(F32)
        step = 2
        while step < owners:
            rows //= 2
            got = swap(total[rows:].astype(BF), "expert", step)
            total = total[:rows] + got.astype(F32)
            step *= 2
        return total

    def column_groups(rows):
        span = rows.shape[1] // groups
        return [rows[:, d * span : (d + 1) * span] for d in range(groups)]

    def attention_grads(grad_low, normed, mixed, grads):
        low_moved = moved(grad_low)
        normed_moved = moved(normed)
        out_part = share_dense([mm(low_moved, m, TN) for m in column_groups(mixed)])
        split = [column_groups(g) for g in grads]
        qkv_part = share_dense(
            [
                mm(normed_moved, jnp.concatenate([s[d] for s in split], 1), TN)
                for d in range(groups)
            ]
        )
        span = qkv_part.shape[1] // 3
        qkv_grad = jnp.stack([qkv_part[:, s * span : (s + 1) * span] for s in range(3)])
        return qkv_grad, out_part.T

    grad_low = grad_second.astype(BF)
    grad_part, grads = attend_backward(grad_low, out_second, qkv_second, saved_second, images)
    qkv_two, out_two = attention_grads(grad_low, normed_second, saved_second[2], grads)
    back, gain_three, bias_three = norm_backward(after_dense, gains[2], biases[2], grad_part)
    grad_dense = grad_second + back
    grad_low = grad_dense.astype(BF)
    grad_hid = [
        (mm(grad_low, w, NT) * s.astype(F32)).astype(BF) for w, s in zip(dense_out, dense_slope)
    ]
    grad_part = sum(mm(g, w, NT) for g, w in zip(grad_hid, dense_in))
    low_moved = moved(grad_low)
    normed_moved = moved(normed_dense)
    grad_mlp_out = share_dense([mm(low_moved, a, TN) for a in dense_act]).T
    grad_mlp_in = share_dense([mm(normed_moved, g, TN) for g in grad_hid])
    back, gain_two, bias_two = norm_backward(after_attn, gains[1], biases[1], grad_part)
    grad_attn = grad_dense + back
    grad_low = grad_attn.astype(BF)
    grad_part, grads = attend_backward(grad_low, out_first, qkv_first, saved_first, images)
    back, gain_one, bias_one = norm_backward(start, gains[0], biases[0], grad_part)
    grad_start = (grad_attn + back).astype(BF)
    start_all = jnp.concatenate(
        [grad_start] + [swap(grad_start, "tensor", d) for d in range(1, groups)], 0
    )
    input_grad = absolute(start_all)
    qkv_one, out_one = attention_grads(grad_low, normed_first, saved_first[2], grads)

    small = jnp.concatenate(
        [
            jnp.stack([gain_one, gain_two, gain_three, gain_four]),
            jnp.stack([bias_one, bias_two, bias_three, bias_four]),
            grad_router,
        ],
        0,
    )
    small = lax.psum_scatter(
        lax.psum(small, "tensor"), "expert", scatter_dimension=1, tiled=True
    )
    return (
        activations,
        input_grad,
        small[:4],
        small[4:7],
        small[7],
        jnp.stack([qkv_one, qkv_two]),
        jnp.stack([out_one, out_two]),
        grad_mlp_in,
        grad_mlp_out,
        small[8:].T,
        grad_expert_in[None],
        grad_expert_out[None],
    )


def solution(mesh):
    in_specs = (
        P("expert", None),
        P("expert", None),
        P("expert"),
        P("expert", None),
        P(),
        P(),
        P(),
        P(None, None, None, "tensor"),
        P(None, "tensor", None),
        P(None, "tensor"),
        P("tensor", None),
        P(),
        P("expert", None, "tensor"),
        P("expert", "tensor", None),
    )
    out_specs = (
        P("expert", None),
        P("expert", None),
        P(None, "expert"),
        P(None, "expert"),
        P("expert"),
        P(None, None, "expert", "tensor"),
        P(None, "tensor", "expert"),
        P("expert", "tensor"),
        P("tensor", "expert"),
        P("expert", None),
        P("expert", None, "tensor"),
        P("expert", "tensor", None),
    )
    return jax.shard_map(body, mesh=mesh, in_specs=in_specs, out_specs=out_specs, check_vma=False)
```

```python
import functools

import jax
import jax.numpy as jnp
from jax import lax
from jax.experimental import pallas as pl
from jax.experimental.pallas import tpu as pltpu
from jax.sharding import PartitionSpec as P

HD = 64
SEQ = 197
ROWS = 208
EPS = 1e-06
COST = 0.2
BF = jnp.bfloat16
F32 = jnp.float32


def mm(a, b, dims):
    return lax.dot_general(a, b, (dims, ((), ())), preferred_element_type=F32)


NN = ((1,), (0,))
NT = ((1,), (1,))
TN = ((0,), (0,))


def swap(value, axis, distance):
    size = lax.axis_size(axis)
    return lax.ppermute(value, axis, [(k, k ^ distance) for k in range(size)])


def gelu_both(x):
    k = 0.7978845608028654
    a = 0.044715 * k
    square = x * x
    half = 0.5 * jnp.tanh(x * (a * square + k)) + 0.5
    act = x * half
    return act, half + act * (1.0 - half) * (6.0 * a * square + 2.0 * k)


def row_stats(values):
    center = values - jnp.mean(values, axis=-1, keepdims=True)
    scale = lax.rsqrt(jnp.mean(center * center, axis=-1, keepdims=True) + EPS)
    return center * scale, scale


def norm_pull(grad, hat, scale, gain):
    inner = grad * gain
    first = jnp.mean(inner, axis=-1, keepdims=True)
    second = jnp.mean(inner * hat, axis=-1, keepdims=True)
    return scale * (inner - first - hat * second)


def attend_copies(layer, place, refs, targets, sems):
    qkv_in, out_in, parts = refs[0], refs[1], refs[2:]
    own_qkv, own_out, far_qkv, far_out = targets
    pairs = [(qkv_in.at[layer], own_qkv), (out_in.at[layer], own_out)]
    blocks, span = far_out.shape[1], far_out.shape[2]
    rows, few = far_qkv.shape[2] // 4, span // 4
    for k, part in enumerate(parts):
        d = k // 4
        quarter = (place % 4) ^ (k % 4)
        at = pl.multiple_of(quarter * rows, 16)
        for s in range(3):
            pairs.append((part.at[pl.ds(s * rows, rows)], far_qkv.at[d, s, pl.ds(at, rows)]))
        at = pl.multiple_of(quarter * few, 16)
        for j in range(blocks):
            source = part.at[pl.ds(3 * rows + j * few, few)]
            pairs.append((source, far_out.at[d, j, pl.ds(at, few)]))
    return [pltpu.make_async_copy(x, y, sems.at[n]) for n, (x, y) in enumerate(pairs)]


def dense_copies(place, refs, targets, sems):
    first_in, second_in, parts = refs[0], refs[1], refs[2:]
    own_first, own_second, far_first, far_second = targets
    pairs = [(first_in, own_first), (second_in, own_second)]
    width, span = own_first.shape
    rows, few = width // 4, span // 4
    for k, part in enumerate(parts):
        d = k // 4
        quarter = (place % 4) ^ (k % 4)
        at = pl.multiple_of(quarter * rows, 16)
        pairs.append((part.at[pl.ds(0, rows)], far_first.at[d, pl.ds(at, rows)]))
        for j in range(few // rows):
            at = pl.multiple_of(quarter * few + j * rows, 16)
            source = part.at[pl.ds(rows, rows), pl.ds(j * width, width)]
            pairs.append((source, far_second.at[d, pl.ds(at, rows)]))
    return [pltpu.make_async_copy(x, y, sems.at[n]) for n, (x, y) in enumerate(pairs)]


def attend_scratch(width, groups):
    span = width // groups
    return (
        (3, width, span), (span, width), (groups - 1, 3, width, span),
        (groups - 1, groups, span, span),
    ), 2 + 4 * (groups - 1) * (3 + groups)


def dense_scratch(width, hidden, groups):
    span = hidden // groups
    return (
        (width, span), (span, width), (groups - 1, width, span), (groups - 1, span, width),
    ), 2 + 4 * (groups - 1) * (1 + span // width)


def run_at_start(copies):
    @pl.when(pl.program_id(0) == 0)
    def _():
        for copy in copies:
            copy.start()


def wait_at_start(copies):
    @pl.when(pl.program_id(0) == 0)
    def _():
        for copy in copies:
            copy.wait()


def pair_masks():
    left = lax.broadcasted_iota(jnp.int32, (ROWS, 2 * HD), 1) < HD
    seen = lax.broadcasted_iota(jnp.int32, (2 * ROWS, ROWS), 1) < SEQ
    return left, seen


def stack_pair(rows, left):
    none = jnp.zeros_like(rows)
    return jnp.concatenate([jnp.where(left, rows, none), jnp.where(left, none, rows)], 0)


def attend_kernel(layer, groups, follow, place_ref, x_ref, gain_ref, bias_ref, *refs):
    next_norm, refs = refs[: 2 * follow], refs[2 * follow :]
    many = 4 * groups - 2
    new_ref, normed_ref, packed_ref, mixed_ref, total_ref = refs[many : many + 5]
    targets, sems = refs[-5:-1], refs[-1]
    next_refs = refs[many + 5 : -5]
    own_qkv, own_out, far_qkv, far_out = targets
    copies = attend_copies(layer, place_ref[0], refs[:many], targets, sems)
    run_at_start(copies)
    values = x_ref[...]
    hat, _ = row_stats(values)
    normed = (hat * gain_ref[...] + bias_ref[...]).astype(BF)
    normed_ref[...] = normed
    wait_at_start(copies)
    span = own_qkv.shape[-1]
    for s in range(3):
        packed_ref[s, :, :span] = mm(normed, own_qkv[s], NN).astype(BF)
        for d in range(1, groups):
            part = mm(normed, far_qkv[d - 1, s], NN).astype(BF)
            packed_ref[s, :, d * span : (d + 1) * span] = part
    left, seen = pair_masks()
    lane = lax.broadcasted_iota(jnp.int32, (ROWS, 128), 1)
    totals = jnp.zeros((ROWS, 128), F32)
    for pair in range(packed_ref.shape[-1] // (2 * HD)):
        cols = slice(pair * 2 * HD, (pair + 1) * 2 * HD)
        query = stack_pair(packed_ref[0, :, cols] * BF(HD**-0.5), left)
        scores = jnp.where(seen, mm(query, packed_ref[1, :, cols], NT), -1e30)
        most = jnp.max(scores, axis=-1, keepdims=True)
        probs = jnp.exp(scores - most)
        total = jnp.sum(probs, axis=-1, keepdims=True)
        mixed = mm(probs.astype(BF), packed_ref[2, :, cols], NN) / total
        mixed_ref[:, cols] = jnp.where(left, mixed[:ROWS], mixed[ROWS:]).astype(BF)
        logs = most + jnp.log(total)
        totals = jnp.where(lane == 2 * pair, logs[:ROWS], totals)
        totals = jnp.where(lane == 2 * pair + 1, logs[ROWS:], totals)
    total_ref[...] = totals
    values = values + mm(mixed_ref[:, :span], own_out[...], NN)
    for d in range(1, groups):
        mixed = mixed_ref[:, d * span : (d + 1) * span]
        parts = [mm(mixed, far_out[d - 1, j], NN) for j in range(groups)]
        values = values + jnp.concatenate(parts, 1)
    new_ref[...] = values
    for next_ref in next_refs:
        hat, _ = row_stats(values)
        next_ref[...] = (hat * next_norm[0][...] + next_norm[1][...]).astype(BF)


def attend_back_kernel(
    layer, groups, place_ref, grad_ref, x_ref, packed_ref, total_ref, gain_ref, *refs
):
    many = 4 * groups - 2
    targets, sems = refs[-5:-1], refs[-1]
    moved_ref, gain_out, bias_out = refs[many : many + 3]
    new_refs = refs[many + 3 : -5]
    own_qkv, own_out, far_qkv, far_out = targets
    copies = attend_copies(layer, place_ref[0], refs[:many], targets, sems)
    run_at_start(copies)
    grad = grad_ref[...]
    low = grad.astype(BF)
    wait_at_start(copies)
    span = own_qkv.shape[-1]
    grad_mixed = [mm(low, own_out[...], NT).astype(BF)]
    for d in range(1, groups):
        parts = [
            mm(low[:, j * span : (j + 1) * span], far_out[d - 1, j], NT) for j in range(groups)
        ]
        grad_mixed.append(sum(parts).astype(BF))
    grad_mixed = jnp.concatenate(grad_mixed, 1)
    left, seen = pair_masks()
    for pair in range(packed_ref.shape[-1] // (2 * HD)):
        cols = slice(pair * 2 * HD, (pair + 1) * 2 * HD)
        query = stack_pair(packed_ref[0, :, cols] * BF(HD**-0.5), left)
        key = packed_ref[1, :, cols]
        outer = stack_pair(grad_mixed[:, cols], left)
        total = jnp.concatenate(
            [total_ref[:, 2 * pair : 2 * pair + 1], total_ref[:, 2 * pair + 1 : 2 * pair + 2]], 0
        )
        probs = jnp.where(seen, jnp.exp(mm(query, key, NT) - total), 0.0)
        grad_probs = mm(outer, packed_ref[2, :, cols], NT)
        inner = jnp.sum(grad_probs * probs, axis=-1, keepdims=True)
        grad_scores = (probs * (grad_probs - inner)).astype(BF)
        grad_query = mm(grad_scores, key, NN) * HD**-0.5
        moved_ref[0, :, cols] = jnp.where(left, grad_query[:ROWS], grad_query[ROWS:]).astype(BF)
        moved_ref[1, :, cols] = mm(grad_scores, query, TN).astype(BF)
        moved_ref[2, :, cols] = mm(probs.astype(BF), outer, TN).astype(BF)
    back = jnp.zeros_like(grad)
    for s in range(3):
        back = back + mm(moved_ref[s, :, :span], own_qkv[s], NT)
        for d in range(1, groups):
            back = back + mm(moved_ref[s, :, d * span : (d + 1) * span], far_qkv[d - 1, s], NT)
    finish_back(grad, back, x_ref, gain_ref, new_refs, gain_out, bias_out)


def finish_back(grad, back, x_ref, gain_ref, new_refs, gain_out, bias_out):
    hat, scale = row_stats(x_ref[...])
    grad = grad + norm_pull(back, hat, scale, gain_ref[...])
    for new_ref in new_refs:
        new_ref[...] = grad.astype(new_ref.dtype)

    @pl.when(pl.program_id(0) == 0)
    def _():
        gain_out[...] = jnp.zeros_like(gain_out)
        bias_out[...] = jnp.zeros_like(bias_out)

    gain_out[...] += jnp.sum(back * hat, axis=0, keepdims=True)
    bias_out[...] += jnp.sum(back, axis=0, keepdims=True)


def dense_kernel(groups, place_ref, x_ref, gain_ref, bias_ref, *refs):
    many = 4 * groups - 2
    new_ref, normed_ref, act_ref, slope_ref = refs[many : many + 4]
    targets, sems = refs[many + 4 : -1], refs[-1]
    copies = dense_copies(place_ref[0], refs[:many], targets, sems)
    firsts = [targets[0]] + [targets[2].at[d] for d in range(groups - 1)]
    seconds = [targets[1]] + [targets[3].at[d] for d in range(groups - 1)]
    run_at_start(copies)
    values = x_ref[...]
    hat, _ = row_stats(values)
    normed = (hat * gain_ref[...] + bias_ref[...]).astype(BF)
    normed_ref[...] = normed
    wait_at_start(copies)
    span = targets[0].shape[-1]
    chunk = span // 2
    for d in range(groups):
        for part in range(2):
            inner = slice(part * chunk, (part + 1) * chunk)
            cols = slice(d * span + part * chunk, d * span + (part + 1) * chunk)
            act, slope = gelu_both(mm(normed, firsts[d][:, inner], NN))
            act = act.astype(BF)
            act_ref[:, cols] = act
            slope_ref[:, cols] = slope.astype(BF)
            values = values + mm(act, seconds[d][inner], NN)
    new_ref[...] = values


def dense_back_kernel(groups, place_ref, grad_ref, x_ref, slope_ref, gain_ref, *refs):
    many = 4 * groups - 2
    moved_ref, gain_out, bias_out = refs[many : many + 3]
    new_refs = refs[many + 3 : -5]
    targets, sems = refs[-5:-1], refs[-1]
    copies = dense_copies(place_ref[0], refs[:many], targets, sems)
    firsts = [targets[0]] + [targets[2].at[d] for d in range(groups - 1)]
    seconds = [targets[1]] + [targets[3].at[d] for d in range(groups - 1)]
    run_at_start(copies)
    grad = grad_ref[...]
    low = grad.astype(BF)
    wait_at_start(copies)
    span = targets[0].shape[-1]
    chunk = span // 2
    back = jnp.zeros_like(grad)
    for d in range(groups):
        for part in range(2):
            inner = slice(part * chunk, (part + 1) * chunk)
            cols = slice(d * span + part * chunk, d * span + (part + 1) * chunk)
            hidden = mm(low, seconds[d][inner], NT) * slope_ref[:, cols].astype(F32)
            hidden = hidden.astype(BF)
            moved_ref[:, cols] = hidden
            back = back + mm(hidden, firsts[d][:, inner], NT)
    finish_back(grad, back, x_ref, gain_ref, new_refs, gain_out, bias_out)


def image_block(*shape):
    lead = len(shape) - 2
    return pl.BlockSpec(shape, lambda i: (0,) * lead + (i, 0))


def fixed_block(*shape):
    return pl.BlockSpec(shape, lambda i: (0,) * len(shape))


RAW = pl.BlockSpec(memory_space=pl.ANY)


def dense_call(kernel, place, rows, singles, flat, outs, scratch, flops):
    buffers, copies = scratch
    specs = [pl.BlockSpec(memory_space=pltpu.SMEM)]
    specs += [image_block(*r.shape[:-2], ROWS, r.shape[-1]) for r in rows]
    specs += [fixed_block(*r.shape) for r in singles]
    specs += [RAW] * len(flat)
    out_specs = [
        image_block(*o.shape[:-2], ROWS, o.shape[-1]) if o.shape[-2] > 1 else fixed_block(*o.shape)
        for o in outs
    ]
    moved = sum(o.size * o.dtype.itemsize for o in list(outs) + list(rows) + flat)
    return pl.pallas_call(
        kernel,
        grid=(rows[0].shape[-2] // ROWS,),
        in_specs=specs,
        out_specs=out_specs,
        out_shape=outs,
        scratch_shapes=[pltpu.VMEM(b, BF) for b in buffers]
        + [pltpu.SemaphoreType.DMA((copies,))],
        cost_estimate=cost_of(flops, moved),
    )(place, *rows, *singles, *flat)


def cost_of(flops, moved):
    return pl.CostEstimate(
        flops=int(COST * flops), bytes_accessed=int(COST * moved), transcendentals=0
    )


def shape(*dims, kind=BF):
    return jax.ShapeDtypeStruct(dims, kind)


def attend_forward(layer, groups, place, values, gain, bias, weights, follow=()):
    rows, width = values.shape
    outs = (
        shape(rows, width, kind=F32),
        shape(rows, width),
        shape(3, rows, width),
        shape(rows, width),
        shape(rows, 128, kind=F32),
    ) + (shape(rows, width),) * bool(follow)
    return dense_call(
        functools.partial(attend_kernel, layer, groups, bool(follow)),
        place, (values,), (gain, bias) + follow, weights, outs, attend_scratch(width, groups),
        rows * width * (8 * width + 4 * ROWS),
    )


def attend_backward(
    layer, groups, place, grad, values, gain, packed, total, weights, kinds
):
    rows, width = values.shape
    outs = (
        shape(3, rows, width),
        shape(1, width, kind=F32),
        shape(1, width, kind=F32),
    ) + tuple(shape(rows, width, kind=k) for k in kinds)
    return dense_call(
        functools.partial(attend_back_kernel, layer, groups),
        place, (grad, values, packed, total), (gain,), weights, outs,
        attend_scratch(width, groups), rows * width * (8 * width + 10 * ROWS),
    )


def dense_forward(groups, place, values, gain, bias, weights):
    rows, width = values.shape
    hidden = groups * weights[0].shape[-1]
    outs = (
        shape(rows, width, kind=F32),
        shape(rows, width),
        shape(rows, hidden),
        shape(rows, hidden),
    )
    return dense_call(
        functools.partial(dense_kernel, groups),
        place, (values,), (gain, bias), weights, outs, dense_scratch(width, hidden, groups),
        4 * rows * width * hidden,
    )


def dense_backward(groups, place, grad, values, gain, slope, weights):
    rows, width = values.shape
    hidden = groups * weights[0].shape[-1]
    outs = (
        shape(rows, hidden),
        shape(1, width, kind=F32),
        shape(1, width, kind=F32),
        shape(rows, width, kind=F32),
        shape(rows, width),
    )
    return dense_call(
        functools.partial(dense_back_kernel, groups),
        place, (grad, values, slope), (gain,), weights, outs,
        dense_scratch(width, hidden, groups), 4 * rows * width * hidden,
    )


def expert_kernel(rows_ref, *refs):
    weights, (out_ref, act_ref, slope_ref) = refs[:-3], refs[-3:]
    rows = rows_ref[...]
    width = rows.shape[1]
    span = weights[0].shape[1]
    total = jnp.zeros(rows.shape, F32)
    for j, weight in enumerate(weights):
        cols = slice(j * span, (j + 1) * span)
        act, slope = gelu_both(mm(rows, weight[:width], NN))
        act = act.astype(BF)
        act_ref[:, cols] = act
        slope_ref[:, cols] = slope.astype(BF)
        parts = [mm(act, weight[k : k + span], NN) for k in range(width, 2 * width, span)]
        total = total + (jnp.concatenate(parts, 1) if len(parts) > 1 else parts[0])
    out_ref[...] = total.astype(BF)


def expert_back_kernel(grad_ref, slope_ref, *refs):
    weights, (out_ref, hidden_ref) = refs[:-2], refs[-2:]
    grad = grad_ref[...]
    width = grad.shape[1]
    span = weights[0].shape[1]
    total = jnp.zeros(grad.shape, F32)
    for j, weight in enumerate(weights):
        cols = slice(j * span, (j + 1) * span)
        parts = [
            mm(grad[:, k : k + span], weight[width + k : width + k + span], NT)
            for k in range(0, width, span)
        ]
        hidden = (sum(parts) * slope_ref[:, cols].astype(F32)).astype(BF)
        hidden_ref[:, cols] = hidden
        total = total + mm(hidden, weight[:width], NT)
    out_ref[...] = total.astype(BF)


def expert_call(kernel, rows, weights, outs):
    count = rows[0].shape[0]
    tile = 256 if count % 256 == 0 else 128
    hold = [
        pl.BlockSpec(w.shape, lambda i: (0, 0), pipeline_mode=pl.Buffered(1)) for w in weights
    ]
    moved = sum(o.size * o.dtype.itemsize for o in list(outs) + list(rows) + list(weights))
    return pl.pallas_call(
        kernel,
        grid=(count // tile,),
        in_specs=[image_spec(tile, r) for r in rows] + hold,
        out_specs=[image_spec(tile, o) for o in outs],
        out_shape=outs,
        cost_estimate=cost_of(2 * count * sum(w.size for w in weights), moved),
    )(*rows, *weights)


def image_spec(tile, like):
    return pl.BlockSpec((tile, like.shape[1]), lambda i: (i, 0))


def expert_forward(rows, weights):
    count, width = rows.shape
    hidden = len(weights) * weights[0].shape[1]
    outs = (shape(count, width), shape(count, hidden), shape(count, hidden))
    return expert_call(expert_kernel, (rows,), weights, outs)


def expert_backward(grad, slope, weights):
    outs = (shape(*grad.shape), shape(*slope.shape))
    return expert_call(expert_back_kernel, (grad, slope), weights, outs)


def weight_kernel(groups, lines, mover_ref, *refs):
    stats, refs = refs[:lines], refs[lines:]
    count = (len(refs) - 2) // 2
    lefts, rights, (keep_ref, send_ref) = refs[:count], refs[count:-2], refs[-2:]
    half = keep_ref.shape[0]
    turned = [mm(mover_ref[...], left[...], NT).astype(BF) for left in lefts]
    at = 0
    columns = keep_ref.shape[1] // groups
    for left, right in zip(turned, rights):
        for s in range(right.shape[0] if len(right.shape) == 3 else 1):
            source = right.at[s] if len(right.shape) == 3 else right
            span = source.shape[1] // groups
            tile = min(source.shape[1], 768)
            for k in range(0, source.shape[1], tile):
                part = mm(left, source[:, k : k + tile], NN).astype(BF)
                for j in range(k, k + tile, min(span, tile)):
                    low = (j // span) * columns + at + j % span
                    high = low + min(span, tile)
                    piece = part[:, j - k : j - k + min(span, tile)]
                    keep_ref[:, low:high] = piece[:half]
                    send_ref[:, low:high] = piece[half:]
            at += span
    if lines:
        rows = [stat[...] for stat in stats]
        room = columns - at
        rows.append(jnp.zeros((room - sum(r.shape[0] for r in rows), half * 2), F32))
        piece = mm(mover_ref[...], jnp.concatenate(rows, 0).astype(BF), NT).astype(BF)
        for d in range(groups):
            keep_ref[:, d * columns + at : (d + 1) * columns] = piece[:half]
            send_ref[:, d * columns + at : (d + 1) * columns] = piece[half:]


def weight_grads(groups, mover, pairs, stats=()):
    width = mover.shape[0]
    columns = sum(r.size // r.shape[-2] for _, r in pairs)
    columns += groups * -(-sum(r.shape[0] for r in stats) // 128) * 128
    out = shape(width // 2, columns)
    rows = pairs[0][0].shape[0]
    operands = [mover, *stats] + [p[0] for p in pairs] + [p[1] for p in pairs]
    return pl.pallas_call(
        functools.partial(weight_kernel, groups, len(stats)),
        in_specs=[pl.BlockSpec(memory_space=pltpu.VMEM)] * len(operands),
        out_specs=[pl.BlockSpec(memory_space=pltpu.VMEM)] * 2,
        out_shape=(out, out),
        cost_estimate=cost_of(
            2 * width * columns * rows, sum(2 * o.size for o in operands) + 4 * out.size
        ),
    )(*operands)


def dispatch_kernel(part, far, back, extra_ref, lines_ref, gates_ref, rows_ref, *refs):
    seats, got, refs = refs[:far], refs[far : 2 * far], refs[2 * far :]
    out_ref = refs[back]
    tile = out_ref.shape[0]
    base = pl.program_id(0) * tile
    ids = base + lax.broadcasted_iota(jnp.int32, (tile, lines_ref.shape[1]), 0)
    first, second = ids == lines_ref[:1], ids == lines_ref[1:]
    total = mm((first | second).astype(F32).astype(BF), rows_ref[...], NN)
    if back:
        gates = jnp.where(first, gates_ref[:1], 0.0) + jnp.where(second, gates_ref[1:], 0.0)
        refs[2][...] = jnp.sum(total * refs[0][...].astype(F32), axis=1, keepdims=True)
        total = total * jnp.sum(gates, axis=1, keepdims=True)
    else:
        line = base + lax.broadcasted_iota(jnp.int32, (tile, 1), 0)
        total = total + jnp.where(line % part == part - 1, extra_ref[0], 0.0)
    for seat, x in zip(seats, got):
        ids = base + lax.broadcasted_iota(jnp.int32, (tile, seat.shape[1]), 0)
        total = total + mm((ids == seat[...]).astype(F32).astype(BF), x[...], NN)
    out_ref[...] = total.astype(BF)


def dispatch_call(part, slots, extra, lines, gates, rows, seats, got, merged=None):
    tile = 256 if slots % 256 == 0 else 128
    width = rows.shape[1]
    back = merged is not None
    held = [lines, gates, rows, *seats, *got]
    block = pl.BlockSpec((tile, width), lambda i: (i, 0))
    outs = (shape(slots, width),)
    specs = (block,)
    if back:
        outs += (shape(slots, 1, kind=F32),)
        specs += (pl.BlockSpec((tile, 1), lambda i: (i, 0)),)
    inputs = held + [merged] * back
    return pl.pallas_call(
        functools.partial(dispatch_kernel, part, len(got), back),
        grid=(slots // tile,),
        in_specs=[pl.BlockSpec(memory_space=pltpu.SMEM)]
        + [fixed_block(*x.shape) for x in held]
        + [block] * back,
        out_specs=specs,
        out_shape=outs,
        cost_estimate=cost_of(2 * slots * rows.size, 2 * (slots * width + rows.size)),
    )(extra, *inputs)


def picks_of(cols_ref, gates_ref, count):
    ids = lax.broadcasted_iota(jnp.int32, (cols_ref.shape[0], count), 1)
    first, second = ids == cols_ref[:, :1], ids == cols_ref[:, 1:]
    if gates_ref is None:
        return (first | second).astype(F32).astype(BF)
    picks = jnp.where(first, gates_ref[:, :1], 0.0) + jnp.where(second, gates_ref[:, 1:], 0.0)
    return picks.astype(BF)


def combine_kernel(far, cols_ref, gates_ref, x_ref, teacher_ref, scale_ref, *refs):
    others, rows_ref, got = refs[:far], refs[far], refs[far + 1 : 2 * far + 1]
    final_ref, grad_ref, low_ref = refs[2 * far + 1 :]
    total = x_ref[...]
    for cols, rows in zip((cols_ref,) + others, (rows_ref,) + got):
        total = total + mm(picks_of(cols, gates_ref, rows.shape[0]), rows[...], NN)
    final_ref[...] = total.astype(BF)
    grad = scale_ref[...] * (total - teacher_ref[...].astype(F32))
    grad_ref[...] = grad
    low_ref[...] = grad.astype(BF)


def combine_back_kernel(far, cols_ref, x_ref, grad_ref, logits_ref, *refs):
    others, rows_ref, got = refs[:far], refs[far], refs[far + 1 : 2 * far + 1]
    router_ref, gain_ref, gain_out, bias_out, *new_refs = refs[2 * far + 1 :]
    total = mm(logits_ref[...], router_ref[...], NT)
    for cols, rows in zip((cols_ref,) + others, (rows_ref,) + got):
        total = total + mm(picks_of(cols, None, rows.shape[0]), rows[...], NN)
    finish_back(grad_ref[...], total, x_ref, gain_ref, new_refs, gain_out, bias_out)


def combine_call(kernel, tiled, held, outs):
    moved = sum(x.size * x.dtype.itemsize for x in list(tiled) + list(held) + list(outs))
    return pl.pallas_call(
        kernel,
        grid=(tiled[0].shape[0] // ROWS,),
        in_specs=[image_block(ROWS, x.shape[1]) for x in tiled]
        + [fixed_block(*x.shape) for x in held],
        out_specs=[
            image_block(ROWS, o.shape[1]) if o.shape[0] > 1 else fixed_block(*o.shape) for o in outs
        ],
        out_shape=outs,
        cost_estimate=cost_of(2 * tiled[0].shape[0] * held[0].size, moved),
    )(*tiled, *held)


def outer_kernel(left_ref, right_ref, *refs):
    part = mm(left_ref[...], right_ref[...], TN)
    for got in refs[:-1]:
        part = part + got[...].astype(F32)
    refs[-1][...] = part.astype(refs[-1].dtype)


def expert_grads(left, right, width, span, odd, got=None, cut_left=True):
    rows = left.shape[0]
    wide = left.shape[1] if cut_left else right.shape[1]
    count = wide // (2 * span)
    high, low = (span, width) if cut_left else (width, span)
    cut = pl.BlockSpec((rows, span), lambda j: (0, 2 * j + odd))
    whole = pl.BlockSpec((rows, width), lambda j: (0, 0))
    block = pl.BlockSpec((high, low), lambda j: (j, 0))
    more = () if got is None else (got,)
    out = shape(count * high, low)
    return pl.pallas_call(
        outer_kernel,
        grid=(count,),
        in_specs=([cut, whole] if cut_left else [whole, cut]) + [block] * len(more),
        out_specs=block,
        out_shape=out,
        cost_estimate=cost_of(2 * out.size * rows, 2 * (left.size + right.size + 2 * out.size)),
    )(left, right, *more)


def pinned_all(values, *others):
    return lax.optimization_barrier(tuple(values) + others)[: len(values)]


def pinned(value, *others):
    return lax.optimization_barrier((value,) + others)[0]


def body(
    tokens,
    teacher,
    valid_flags,
    routes,
    capacity,
    norm_gains,
    norm_biases,
    attn_qkv,
    attn_out,
    mlp_in,
    mlp_out,
    router,
    expert_in,
    expert_out,
):
    owners = lax.axis_size("expert")
    groups = lax.axis_size("tensor")
    place = lax.axis_index("expert")
    group = lax.axis_index("tensor")
    local_rows, width = tokens.shape
    experts = router.shape[1]
    image_count = local_rows // SEQ
    images = -(-image_count // groups)
    own_rows = images * ROWS
    all_rows = groups * own_rows
    capacity_most = 4 * (3 * local_rows // (4 * experts))
    used = -(-capacity_most // (2 * groups))
    part = -(-(used + 1) // 16) * 16
    slots = owners * part
    gains = norm_gains.astype(F32)
    biases = norm_biases.astype(F32)

    def relative(rows, fill, count):
        shape = rows.shape[1:]
        grid = rows.reshape((image_count, SEQ) + shape)
        grid = jnp.pad(
            grid,
            [(0, groups * images - image_count), (0, ROWS - SEQ)] + [(0, 0)] * len(shape),
            constant_values=fill,
        )
        taken = [
            lax.dynamic_slice_in_dim(grid, (group ^ d) * images, images, 0) for d in range(count)
        ]
        return jnp.concatenate(taken, 0).reshape((count * own_rows,) + shape)

    def absolute(rows):
        shape = rows.shape[1:]
        grid = rows.reshape((groups * images, ROWS) + shape)
        taken = [
            lax.dynamic_slice_in_dim(grid, (group ^ d) * images, images, 0) for d in range(groups)
        ]
        grid = jnp.concatenate(taken, 0)[:image_count, :SEQ]
        return grid.reshape((local_rows,) + shape)

    place_ref = jnp.full((1,), place, jnp.int32)
    gain_rows = [gains[j : j + 1] for j in range(4)]
    bias_rows = [biases[j : j + 1] for j in range(4)]

    quarter = place % 4

    def attend_piece(layer):
        span = attn_out.shape[1]
        rows, few = width // 4, span // 4
        qkv_part = lax.dynamic_slice(
            attn_qkv, (layer, 0, quarter * rows, 0), (1, 3, rows, span)
        ).reshape(3 * rows, span)
        out_part = lax.dynamic_slice(attn_out, (layer, quarter * few, 0), (1, few, width))[0]
        parts = [out_part[:, j * span : (j + 1) * span] for j in range(groups)]
        return jnp.concatenate([qkv_part] + parts, 0)

    def dense_piece(first, second):
        rows, few = width // 4, second.shape[0] // 4
        second = lax.dynamic_slice_in_dim(second, quarter * few, few, 0)
        parts = [second[j * rows : (j + 1) * rows] for j in range(few // rows)]
        first = lax.dynamic_slice_in_dim(first, quarter * rows, rows, 0)
        return jnp.concatenate([first, jnp.concatenate(parts, 1)], 0)

    def over_tensor(value):
        return [swap(value, "tensor", d) for d in range(1, groups)]

    def both_cores(value):
        return [value, swap(value, "expert", 1)]

    last = [None]

    def after(*values):
        if last[0] is not None:
            values = pinned_all(values, last[0])
        return values if len(values) > 1 else values[0]

    def mark(value):
        last[0] = value
        return value

    def spread(parts):
        return [swap(part, "expert", 2) for part in parts], [swap(part, "expert", 1) for part in parts]

    def fourth(parts):
        return [swap(part, "expert", 1) for part in parts]

    def joined(first, second, third, last):
        return [x for four in zip(first, third, second, last) for x in four]

    piece_first = mark(attend_piece(0))
    first_x = over_tensor(piece_first)
    tokens = after(tokens)
    start = relative(tokens, 0, 1).astype(F32)
    first_x = list(pinned_all(first_x, start))
    first_y, first_c = spread(first_x)
    mark(first_x[0])
    piece_dense = mark(dense_piece(*after(mlp_in, mlp_out)))
    dense_x = over_tensor(piece_dense)
    first_y = list(pinned_all(first_y, piece_dense))
    first_l = fourth(first_y)
    mark(first_y[0])
    piece_second = mark(after(attend_piece(1)))
    second_x = over_tensor(piece_second)
    weights_first = [attn_qkv, attn_out] + joined(first_x, first_y, first_c, first_l)

    room = 2 * used
    kind = jnp.int32
    routes = pinned(routes, first_x[0])
    expert_of = jnp.concatenate([routes[:, 0], routes[:, 1]])
    owner = jnp.tile(jnp.arange(local_rows, dtype=kind) // (SEQ * images), 2)
    of_expert = (expert_of[:, None] == jnp.arange(experts, dtype=kind)).astype(kind)
    of_owner = (owner[:, None] == jnp.arange(groups, dtype=kind)).astype(kind)
    both = (
        (expert_of * groups + owner)[:, None] == jnp.arange(experts * groups, dtype=kind)
    ).astype(kind)
    earlier = (jnp.cumsum(both, axis=0) - both).reshape(-1, experts, groups)
    ahead = jnp.sum(earlier * of_expert[:, :, None], axis=1)
    rank = jnp.sum(ahead * of_owner, axis=1)
    kept_mask = jnp.sum(ahead, axis=1) < jnp.sum(of_expert * capacity[None, :], axis=1)
    held = jnp.sum(both * kept_mask[:, None].astype(kind), axis=0).reshape(experts, groups)
    inside = jnp.minimum(held, room)
    beyond = held - inside
    free = room - inside

    def before(counts):
        return jnp.cumsum(counts, axis=1) - counts

    def of_pair(table):
        return jnp.sum(of_expert[:, :, None] * table[None], axis=1)

    late = jnp.sum(of_pair(before(beyond)) * of_owner, axis=1) + rank - room
    free_from = of_pair(before(free))
    hit = (late[:, None] >= free_from) & (late[:, None] < free_from + of_pair(free))
    hit = hit.astype(kind)
    fits = rank < room
    at = jnp.where(fits, rank, jnp.sum(hit * (of_pair(inside) + late[:, None] - free_from), axis=1))
    home = jnp.where(fits, owner, jnp.sum(hit * jnp.arange(groups, dtype=kind), axis=1))
    row_of = (2 * expert_of + at // used) * part + at % used

    def own_pairs(values):
        return relative(values.reshape(2, local_rows).T, -1, 1)

    local_row = own_pairs(jnp.where(kept_mask & (owner == group) & (home == group), row_of, -1))
    most = min(experts, 2 * SEQ * images // capacity_most)
    rest = min(2 * SEQ * images - most * capacity_most, capacity_most) - room
    most = most * (capacity_most - room) + max(rest, 0)
    most = -(-most // 16) * 16
    few = min(64, most)
    masks = []
    for d in range(1, groups):
        masks.append(kept_mask & (owner == group) & (home == group ^ d))
        masks.append(kept_mask & (owner == group ^ d) & (home == group))
    masks = jnp.stack(masks, 1).astype(kind)
    ranks = jnp.cumsum(masks, axis=0) - masks
    ranks = jnp.where(masks > 0, ranks, -1)
    guest_out, guest_in = [], []
    for d in range(1, groups):
        guest_out.append(own_pairs(ranks[:, 2 * d - 2]))
        named = ranks[:, 2 * d - 1][None, :] == jnp.arange(most, dtype=kind)[:, None]
        guest_in.append(jnp.sum(jnp.where(named, row_of[None, :] + 1, 0), axis=1) - 1)
    distances = [1 << k for k in range(owners.bit_length() - 1)]

    def wider(value, step, *others):
        got = swap(value, "expert", step)
        return jnp.maximum(value, pinned(got, *others) if others else got)

    crowd = wider(jnp.full((8, 128), jnp.max(beyond.sum(0)), kind), 1)
    routes_own = relative(routes, 0, 1)
    valid_rows = relative(jnp.repeat(valid_flags.astype(F32), SEQ)[:, None], 0, 1)

    dense_x = list(pinned_all(dense_x, piece_second, local_row, crowd, *first_c, *first_l))
    dense_y, dense_c = spread(dense_x)
    start = pinned(start, *dense_x)
    after_attn, normed_first, packed_first, mixed_first, total_first = attend_forward(
        0, groups, place_ref, start, gain_rows[0], bias_rows[0], weights_first
    )
    crowd = wider(crowd, 4, after_attn)
    second_x = pinned_all(second_x, after_attn)
    dense_y = pinned_all(dense_y, *second_x)
    dense_l = fourth(dense_y)
    second_y, second_c = spread(second_x)
    weights_dense = [mlp_in, mlp_out] + joined(dense_x, dense_y, dense_c, dense_l)
    after_dense, normed_dense, dense_act, dense_slope = dense_forward(
        groups, place_ref, pinned(after_attn, crowd, *second_x), gain_rows[1], bias_rows[1], weights_dense
    )
    second_y = pinned_all(second_y, after_dense)
    weights_second = [attn_qkv, attn_out] + joined(second_x, second_y, second_c, fourth(second_y))
    crowd = wider(crowd, 8, after_dense)
    second = attend_forward(
        1, groups, place_ref, pinned(after_dense, crowd), gain_rows[2], bias_rows[2],
        weights_second, (gain_rows[3], bias_rows[3]),
    )
    after_second, normed_second, packed_second, mixed_second, total_second, normed_expert = second
    for step in [2] + distances[4:]:
        crowd = wider(crowd, step, after_second)
    logits = mm(normed_expert, router, NN)
    picker = routes_own[:, :, None] == jnp.arange(experts, dtype=kind)[None, None, :]
    chosen = jnp.sum(jnp.where(picker, logits[:, None, :], 0.0), axis=2)
    gate_vals = jax.nn.softmax(chosen, axis=1)
    gate_lines = gate_vals.T
    local_lines = local_row.T
    slot_ids = jnp.arange(slots, dtype=kind)

    def guests(count):
        ids = jnp.arange(count, dtype=kind)[:, None]
        return [(ids == g[None, :, 0], ids == g[None, :, 1]) for g in guest_out]

    def chosen_rows(count, rows):
        return [mm((a | b).astype(BF), rows, NN) for a, b in guests(count)]

    def returned_rows(count, rows):
        return [
            mm((g[:count, None] == slot_ids[None, :]).astype(BF), rows, NN).astype(BF)
            for g in guest_in
        ]

    def seats(count):
        return [g[None, :count] for g in guest_in]

    def over(rows):
        return [swap(x, "tensor", d + 1) for d, x in enumerate(rows)]

    def sized(branch, *operands):
        if few == most:
            return branch(few)(*operands)
        return lax.cond(crowd[0, 0] <= few, branch(few), branch(most), *operands)

    def grown(rows):
        return jnp.pad(rows, ((0, most - rows.shape[0]), (0, 0)))

    def across(rows):
        return lax.all_to_all(
            rows.reshape(owners, part, width), "expert", split_axis=0, concat_axis=0, tiled=True
        ).reshape(slots, width)

    images_valid = jnp.sum(valid_flags.astype(F32)).reshape(1)
    blank = jnp.zeros((2, own_rows), F32)

    def dispatch(count):
        def branch(rows):
            got = over([x.astype(BF) for x in chosen_rows(count, rows)])
            return dispatch_call(
                part, slots, images_valid, local_lines, blank, rows, seats(count), got
            )[0]

        return branch

    sent_rows = sized(dispatch, normed_expert)
    span = expert_in.shape[2]
    blocks = [expert_out[0, :, k : k + span] for k in range(0, width, span)]
    expert_own = pinned(jnp.concatenate([expert_in[0]] + blocks, 0), sent_rows)
    expert_parts = [x for w in [expert_own] + over_tensor(expert_own) for x in both_cores(w)]
    rows_in = across(sent_rows)
    valid_count = SEQ * jnp.sum(rows_in[part - 1 :: part, :1].astype(F32))
    teacher_rel = relative(teacher, 0, 1)
    scale = (local_rows * owners / valid_count) * valid_rows
    rows_in = pinned(rows_in, teacher_rel, scale)
    expert_rows, act, slope = expert_forward(rows_in, expert_parts)
    merged = across(expert_rows)

    outs = (shape(own_rows, width), shape(own_rows, width, kind=F32), shape(own_rows, width))

    def combine(count):
        def branch(rows):
            got = over(returned_rows(count, rows))
            results = combine_call(
                functools.partial(combine_kernel, groups - 1),
                (local_row, gate_vals, after_second, teacher_rel, scale, *guest_out),
                (rows, *got),
                outs,
            )
            return tuple(results) + tuple(grown(x) for x in got)

        return branch

    final_low, grad_final, grad_low, *lodged = sized(combine, merged)

    def dispatch_back(count):
        def branch(rows, merged, *lodged):
            sent, parts = [], []
            for (a, b), x, taken in zip(guests(count), lodged, chosen_rows(count, rows)):
                gates = jnp.sum(
                    jnp.where(a, gate_lines[:1], 0.0) + jnp.where(b, gate_lines[1:], 0.0),
                    axis=1,
                    keepdims=True,
                )
                sent.append((gates * taken).astype(BF))
                inner = jnp.sum(taken * x[:count].astype(F32), axis=1, keepdims=True)
                parts.append(grown(inner))
            results = dispatch_call(
                part, slots, images_valid, local_lines, gate_lines, rows, seats(count),
                over(sent), merged,
            )
            return tuple(results) + tuple(parts)

        return branch

    sent_back, grad_slot_gate, *grad_guest_gate = sized(
        dispatch_back, grad_low, merged, *lodged
    )
    final_far = over_tensor(pinned(final_low, sent_back))
    grad_out_rows = across(sent_back)
    grad_rows, grad_hidden = expert_backward(
        pinned(grad_out_rows, *final_far), slope, expert_parts
    )
    activations = absolute(jnp.concatenate([final_low] + list(pinned_all(final_far, grad_rows)), 0))
    grad_back = across(grad_rows)

    def start_groups(total):
        span = total.shape[1] // groups
        sent = [total[:, d * span : (d + 1) * span].astype(BF) for d in range(1, groups)]
        return total[:, :span], sent

    def start_rows(total):
        rows = total.shape[0] // 2
        return total[:rows], [total[rows:].astype(BF)]

    def cross(sent):
        return [swap(x, "tensor", d + 1) for d, x in enumerate(sent)]

    def along(sent, distance):
        return [swap(x, "expert", distance) for x in sent]

    def finish(keep, got, *after):
        total = keep.astype(F32)
        for x in got:
            total = total + (pinned(x, *after) if after else x).astype(F32)
        return total

    act, rows_in, grad_slot_gate = pinned_all((act, rows_in, grad_slot_gate), grad_rows)
    grad_own = []
    for choice in range(2):
        taken = slot_ids[:, None] == local_row[None, :, choice]
        total = jnp.sum(jnp.where(taken, grad_slot_gate, 0.0), axis=0)
        for pair, values in zip(guests(most), grad_guest_gate):
            total = total + jnp.sum(jnp.where(pair[choice], values, 0.0), axis=0)
        grad_own.append(total)
    grad_own = jnp.stack(grad_own, 1)
    span = expert_in.shape[2]
    sent = mark(expert_grads(act, grad_out_rows, width, span, 1))
    got_eo = along([sent], 1)[0]
    sent = mark(expert_grads(after(rows_in), grad_hidden, width, span, 1, None, False))
    got_ei = along([sent], 1)[0]

    def shares_of(total, rows):
        return total[:rows], [total[d * rows : (d + 1) * rows] for d in range(1, groups)]

    keep_eo, sent_eo = shares_of(
        mark(expert_grads(act, grad_out_rows, width, span, 0, after(got_eo))), span
    )
    got_eo = cross(sent_eo)
    keep_ei, sent_ei = shares_of(
        mark(expert_grads(rows_in, grad_hidden, width, span, 0, after(got_ei), False)), width
    )

    own_gates = gate_vals
    grad_chosen = own_gates * (grad_own - jnp.sum(own_gates * grad_own, axis=1, keepdims=True))
    grad_logits = jnp.sum(
        jnp.where(picker, grad_chosen[:, :, None], 0.0), axis=1
    ).astype(BF)
    grad_router = mm(grad_logits, normed_expert, TN)
    grad_back = pinned(grad_back, *sent_ei, *got_eo, grad_router)
    grad_expert_out = finish(keep_eo, got_eo)

    outs = (shape(1, width, kind=F32),) * 2 + (
        shape(own_rows, width, kind=F32), shape(own_rows, width),
    )

    def combine_back(count):
        def branch(rows):
            results = combine_call(
                functools.partial(combine_back_kernel, groups - 1),
                (local_row, after_second, grad_final, grad_logits, *guest_out),
                (rows, *over(returned_rows(count, rows)), router, gain_rows[3]),
                outs,
            )
            return tuple(results)

        return branch

    gain_four, bias_four, grad_second, low_second = sized(combine_back, grad_back)
    got_ei = cross([pinned(p, grad_second) for p in sent_ei])

    block = width // owners
    feature = jnp.arange(width, dtype=jnp.int32)

    def mover_of(distances):
        ahead, turned = feature // block, 0
        for distance in reversed(distances):
            turned = turned + distance * (ahead % 2)
            ahead = ahead // 2
        source = (turned ^ place) * block + feature % block
        return (source[:, None] == feature[None, :]).astype(BF)

    mover = mover_of(distances)
    turned_order = [1, 4, 2] + distances[3:]
    mover_turned = mover_of(turned_order)

    mark(grad_second)
    def arrive(keep, got):
        return finish(keep, [after(x) for x in got])

    grads_second, gain_three, bias_three, grad_dense, low_dense = attend_backward(
        1, groups, place_ref, grad_second, after_dense, gain_rows[2], packed_second,
        total_second, weights_second, (F32, BF),
    )
    mark(grad_dense)
    got_ei = [after(x) for x in got_ei]
    keep_a, send_a = weight_grads(
        groups,
        mover,
        [(pinned(normed_second, *got_ei), grads_second), (low_second, mixed_second)],
    )
    mark(send_a)
    got_a = along([send_a], 1)
    low_dense = after(low_dense)
    keep_b, send_b = weight_grads(groups, mover, [(low_dense, dense_act)])
    mark(send_b)
    got_b = along([send_b], 1)
    keep_a, sent_a = start_groups(arrive(keep_a, got_a).astype(BF))
    mark(sent_a[0])
    got_a = cross(sent_a)
    grad_expert_in = finish(keep_ei, got_ei)
    grad_hidden, gain_two, bias_two, grad_attn, low_first = dense_backward(
        groups, place_ref, after(grad_dense), after_attn, gain_rows[1], dense_slope, weights_dense,
    )
    mark(grad_attn)
    keep_b, sent_b = start_rows(arrive(keep_b, got_b).astype(BF))
    mark(sent_b[0])
    got_b = along(sent_b, 2)

    got_a = [after(x) for x in got_a]
    stats = [gain_two, gain_three, gain_four, bias_two, bias_three, bias_four]
    keep_c, send_c = weight_grads(
        groups,
        mover_turned,
        [
            (pinned(normed_dense, *got_a), grad_hidden),
            (low_first, mixed_first),
        ],
        stats + [grad_router],
    )
    mark(send_c)
    got_c = along([send_c], 1)
    keep_a, sent_a = start_rows(arrive(keep_a, got_a).astype(BF))
    mark(sent_a[0])
    got_a = along(sent_a, 2)
    keep_c, sent_c = start_rows(arrive(keep_c, got_c).astype(BF))
    mark(sent_c[0])
    got_c = along(sent_c, 4)
    grads_first, gain_one, bias_one, grad_start = attend_backward(
        0, groups, place_ref, after(grad_attn), start, gain_rows[0], packed_first, total_first,
        weights_first, (BF,),
    )
    mark(grad_start)
    start_far = over_tensor(grad_start)
    got_b = [after(x) for x in got_b]
    keep_d, send_d = weight_grads(
        groups,
        mover,
        [(pinned(normed_first, *got_b), grads_first)],
        [gain_one, bias_one],
    )
    mark(send_d)
    got_d = along([send_d], 1)
    keep_b, sent_b = start_groups(arrive(keep_b, got_b).astype(BF))
    mark(sent_b[0])
    got_b = cross(sent_b)
    keep_a, sent_a = start_rows(arrive(keep_a, got_a))
    mark(sent_a[0])
    got_a = along(sent_a, 4)
    total_c = mark(arrive(keep_c, got_c).astype(BF))
    total_d = arrive(keep_d, got_d).astype(BF)
    span = total_d.shape[1] // groups
    cut = attn_out.shape[1]
    far_d = [
        jnp.concatenate([total_d[:, d * span : d * span + cut] for d in range(groups)], 1),
        jnp.concatenate([total_d[:, d * span + cut : (d + 1) * span] for d in range(groups)], 1),
    ]
    keep_d, sent_d = start_groups(far_d[0])
    keep_e, sent_e = start_rows(far_d[1])
    mark(sent_e[0])
    got_d = cross(sent_d)
    got_e = along(sent_e, 2)
    keep_c, sent_c = start_rows(after(total_c))
    mark(sent_c[0])
    got_c = along(sent_c, 2)
    start_far = [after(x) for x in start_far]
    input_grad = mark(absolute(jnp.concatenate([grad_start] + start_far, 0)))
    keep_a, sent_a = start_rows(arrive(keep_a, got_a))
    mark(sent_a[0])
    got_a = along(sent_a, 8)
    keep_b, sent_b = start_rows(arrive(keep_b, got_b))
    mark(sent_b[0])
    got_b = along(sent_b, 4)
    keep_d, sent_d = start_rows(arrive(keep_d, got_d))
    mark(sent_d[0])
    got_d = along(sent_d, 2)
    keep_e, sent_e = start_groups(arrive(keep_e, got_e))
    mark(sent_e[0])
    got_e = cross(sent_e)
    keep_c, sent_c = start_groups(arrive(keep_c, got_c))
    mark(sent_c[0])
    got_c = cross(sent_c)
    total_a = mark(arrive(keep_a, got_a))
    keep_b, sent_b = start_rows(arrive(keep_b, got_b))
    mark(sent_b[0])
    got_b = along(sent_b, 8)
    total_d = arrive(keep_d, got_d)
    total_e = arrive(keep_e, got_e)
    keep_d, sent_d = start_rows(jnp.concatenate([total_d, total_e], 1))
    mark(sent_d[0])
    got_d = along(sent_d, 4)
    keep_c, sent_c = start_rows(arrive(keep_c, got_c))
    mark(sent_c[0])
    got_c = along(sent_c, 8)
    total_b = mark(arrive(keep_b, got_b))
    keep_d, sent_d = start_rows(arrive(keep_d, got_d))
    mark(sent_d[0])
    got_d = along(sent_d, 8)
    total_c = mark(arrive(keep_c, got_c))
    total_d = arrive(keep_d, got_d)
    joint = jnp.concatenate([total_a, total_b, total_c, total_d], 1)
    step = 16
    while step < owners:
        keep, sent = start_rows(joint)
        joint = finish(keep, along(sent, step))
        step *= 2
    spans = [attn_out.shape[1], mlp_in.shape[1], -(-(6 + experts) // 128) * 128]
    widths = [4 * spans[0], spans[1], spans[1], spans[0], spans[2], 3 * spans[0], 128]
    taken, at = [], 0
    for span in widths:
        taken.append(joint[:, at : at + span])
        at += span
    two, grad_mlp_out, grad_mlp_in = taken[0], taken[1].T, taken[2]
    one = jnp.concatenate([taken[5], taken[3]], 1)
    lines, last_lines = taken[4], taken[6]
    joint_small = jnp.concatenate(
        [last_lines[:, :1], lines[:, :3], last_lines[:, 1:2], lines[:, 3 : 6 + experts]], 1
    )

    def split_attention(total):
        span = total.shape[1] // 4
        return jnp.stack([total[:, s * span : (s + 1) * span] for s in range(3)]), total[:, -span:].T

    qkv_one, out_one = split_attention(one)
    qkv_two, out_two = split_attention(two)
    small = joint_small.T
    return (
        activations,
        input_grad,
        small[:4],
        small[4:7],
        small[7],
        jnp.stack([qkv_one, qkv_two]),
        jnp.stack([out_one, out_two]),
        grad_mlp_in,
        grad_mlp_out,
        small[8:].T,
        grad_expert_in[None],
        grad_expert_out[None],
    )


def solution(mesh):
    in_specs = (
        P("expert", None),
        P("expert", None),
        P("expert"),
        P("expert", None),
        P(),
        P(),
        P(),
        P(None, None, None, "tensor"),
        P(None, "tensor", None),
        P(None, "tensor"),
        P("tensor", None),
        P(),
        P("expert", None, "tensor"),
        P("expert", "tensor", None),
    )
    out_specs = (
        P("expert", None),
        P("expert", None),
        P(None, "expert"),
        P(None, "expert"),
        P("expert"),
        P(None, None, "expert", "tensor"),
        P(None, "tensor", "expert"),
        P("expert", "tensor"),
        P("tensor", "expert"),
        P("expert", None),
        P("expert", None, "tensor"),
        P("expert", "tensor", None),
    )
    return jax.shard_map(body, mesh=mesh, in_specs=in_specs, out_specs=out_specs, check_vma=False)
```

```python
import functools

import jax
import jax.numpy as jnp
from jax import lax
from jax.experimental import pallas as pl
from jax.experimental.pallas import tpu as pltpu
from jax.sharding import PartitionSpec as P

HD = 64
SEQ = 197
ROWS = 208
EPS = 1e-06
COST = 0.2
BF = jnp.bfloat16
F32 = jnp.float32


def mm(a, b, dims):
    return lax.dot_general(a, b, (dims, ((), ())), preferred_element_type=F32)


NN = ((1,), (0,))
NT = ((1,), (1,))
TN = ((0,), (0,))


def swap(value, axis, distance):
    size = lax.axis_size(axis)
    return lax.ppermute(value, axis, [(k, k ^ distance) for k in range(size)])


def gelu_both(x):
    k = 0.7978845608028654
    a = 0.044715 * k
    square = x * x
    half = 0.5 * jnp.tanh(x * (a * square + k)) + 0.5
    act = x * half
    return act, half + act * (1.0 - half) * (6.0 * a * square + 2.0 * k)


def row_stats(values):
    center = values - jnp.mean(values, axis=-1, keepdims=True)
    scale = lax.rsqrt(jnp.mean(center * center, axis=-1, keepdims=True) + EPS)
    return center * scale, scale


def norm_pull(grad, hat, scale, gain):
    inner = grad * gain
    first = jnp.mean(inner, axis=-1, keepdims=True)
    second = jnp.mean(inner * hat, axis=-1, keepdims=True)
    return scale * (inner - first - hat * second)


def attend_copies(layer, place, refs, targets, sems):
    qkv_in, out_in, parts = refs[0], refs[1], refs[2:]
    own_qkv, own_out, far_qkv, far_out = targets
    pairs = [(qkv_in.at[layer], own_qkv), (out_in.at[layer], own_out)]
    blocks, span = far_out.shape[1], far_out.shape[2]
    rows, few = far_qkv.shape[2] // 4, span // 4
    for k, part in enumerate(parts):
        d = k // 4
        quarter = (place % 4) ^ (k % 4)
        at = pl.multiple_of(quarter * rows, 16)
        for s in range(3):
            pairs.append((part.at[pl.ds(s * rows, rows)], far_qkv.at[d, s, pl.ds(at, rows)]))
        at = pl.multiple_of(quarter * few, 16)
        for j in range(blocks):
            source = part.at[pl.ds(3 * rows + j * few, few)]
            pairs.append((source, far_out.at[d, j, pl.ds(at, few)]))
    return [pltpu.make_async_copy(x, y, sems.at[n]) for n, (x, y) in enumerate(pairs)]


def dense_copies(place, refs, targets, sems):
    first_in, second_in, parts = refs[0], refs[1], refs[2:]
    own_first, own_second, far_first, far_second = targets
    pairs = [(first_in, own_first), (second_in, own_second)]
    quarters = (place % 4, place % 2 + place // 4 % 2 * 2)
    count = len(parts) // 2
    for k in range(count):
        for side, target in enumerate((far_first, far_second)):
            rows = target.shape[1] // 4
            at = pl.multiple_of((quarters[side] ^ (k % 4)) * rows, 16)
            pairs.append((parts[side * count + k], target.at[k // 4, pl.ds(at, rows)]))
    return [pltpu.make_async_copy(x, y, sems.at[n]) for n, (x, y) in enumerate(pairs)]


def attend_scratch(width, groups):
    span = width // groups
    return (
        (3, width, span), (span, width), (groups - 1, 3, width, span),
        (groups - 1, groups, span, span),
    ), 2 + 4 * (groups - 1) * (3 + groups)


def dense_scratch(width, hidden, groups):
    span = hidden // groups
    return (
        (width, span), (span, width), (groups - 1, width, span), (groups - 1, span, width),
    ), 2 + 8 * (groups - 1)


def run_at_start(copies):
    @pl.when(pl.program_id(0) == 0)
    def _():
        for copy in copies:
            copy.start()


def wait_at_start(copies):
    @pl.when(pl.program_id(0) == 0)
    def _():
        for copy in copies:
            copy.wait()


def pair_masks():
    left = lax.broadcasted_iota(jnp.int32, (ROWS, 2 * HD), 1) < HD
    seen = lax.broadcasted_iota(jnp.int32, (2 * ROWS, ROWS), 1) < SEQ
    return left, seen


def stack_pair(rows, left):
    none = jnp.zeros_like(rows)
    return jnp.concatenate([jnp.where(left, rows, none), jnp.where(left, none, rows)], 0)


def attend_kernel(layer, groups, follow, place_ref, x_ref, gain_ref, bias_ref, *refs):
    next_norm, refs = refs[: 2 * follow], refs[2 * follow :]
    many = 4 * groups - 2
    new_ref, normed_ref, packed_ref, mixed_ref, total_ref = refs[many : many + 5]
    targets, sems = refs[-5:-1], refs[-1]
    next_refs = refs[many + 5 : -5]
    own_qkv, own_out, far_qkv, far_out = targets
    copies = attend_copies(layer, place_ref[0], refs[:many], targets, sems)
    run_at_start(copies)
    values = x_ref[...]
    hat, _ = row_stats(values)
    normed = (hat * gain_ref[...] + bias_ref[...]).astype(BF)
    normed_ref[...] = normed
    wait_at_start(copies)
    span = own_qkv.shape[-1]
    for s in range(3):
        packed_ref[s, :, :span] = mm(normed, own_qkv[s], NN).astype(BF)
        for d in range(1, groups):
            part = mm(normed, far_qkv[d - 1, s], NN).astype(BF)
            packed_ref[s, :, d * span : (d + 1) * span] = part
    left, seen = pair_masks()
    lane = lax.broadcasted_iota(jnp.int32, (ROWS, 128), 1)
    totals = jnp.zeros((ROWS, 128), F32)
    for pair in range(packed_ref.shape[-1] // (2 * HD)):
        cols = slice(pair * 2 * HD, (pair + 1) * 2 * HD)
        query = stack_pair(packed_ref[0, :, cols] * BF(HD**-0.5), left)
        scores = jnp.where(seen, mm(query, packed_ref[1, :, cols], NT), -1e30)
        most = jnp.max(scores, axis=-1, keepdims=True)
        probs = jnp.exp(scores - most)
        total = jnp.sum(probs, axis=-1, keepdims=True)
        mixed = mm(probs.astype(BF), packed_ref[2, :, cols], NN) / total
        mixed_ref[:, cols] = jnp.where(left, mixed[:ROWS], mixed[ROWS:]).astype(BF)
        logs = most + jnp.log(total)
        totals = jnp.where(lane == 2 * pair, logs[:ROWS], totals)
        totals = jnp.where(lane == 2 * pair + 1, logs[ROWS:], totals)
    total_ref[...] = totals
    values = values + mm(mixed_ref[:, :span], own_out[...], NN)
    for d in range(1, groups):
        mixed = mixed_ref[:, d * span : (d + 1) * span]
        parts = [mm(mixed, far_out[d - 1, j], NN) for j in range(groups)]
        values = values + jnp.concatenate(parts, 1)
    new_ref[...] = values
    for next_ref in next_refs:
        hat, _ = row_stats(values)
        next_ref[...] = (hat * next_norm[0][...] + next_norm[1][...]).astype(BF)


def attend_back_kernel(
    layer, groups, place_ref, grad_ref, x_ref, packed_ref, total_ref, gain_ref, *refs
):
    many = 4 * groups - 2
    targets, sems = refs[-5:-1], refs[-1]
    moved_ref, gain_out, bias_out = refs[many : many + 3]
    new_refs = refs[many + 3 : -5]
    own_qkv, own_out, far_qkv, far_out = targets
    copies = attend_copies(layer, place_ref[0], refs[:many], targets, sems)
    run_at_start(copies)
    grad = grad_ref[...]
    low = grad.astype(BF)
    wait_at_start(copies)
    span = own_qkv.shape[-1]
    grad_mixed = [mm(low, own_out[...], NT).astype(BF)]
    for d in range(1, groups):
        parts = [
            mm(low[:, j * span : (j + 1) * span], far_out[d - 1, j], NT) for j in range(groups)
        ]
        grad_mixed.append(sum(parts).astype(BF))
    grad_mixed = jnp.concatenate(grad_mixed, 1)
    left, seen = pair_masks()
    for pair in range(packed_ref.shape[-1] // (2 * HD)):
        cols = slice(pair * 2 * HD, (pair + 1) * 2 * HD)
        query = stack_pair(packed_ref[0, :, cols] * BF(HD**-0.5), left)
        key = packed_ref[1, :, cols]
        outer = stack_pair(grad_mixed[:, cols], left)
        total = jnp.concatenate(
            [total_ref[:, 2 * pair : 2 * pair + 1], total_ref[:, 2 * pair + 1 : 2 * pair + 2]], 0
        )
        probs = jnp.where(seen, jnp.exp(mm(query, key, NT) - total), 0.0)
        grad_probs = mm(outer, packed_ref[2, :, cols], NT)
        inner = jnp.sum(grad_probs * probs, axis=-1, keepdims=True)
        grad_scores = (probs * (grad_probs - inner)).astype(BF)
        grad_query = mm(grad_scores, key, NN) * HD**-0.5
        moved_ref[0, :, cols] = jnp.where(left, grad_query[:ROWS], grad_query[ROWS:]).astype(BF)
        moved_ref[1, :, cols] = mm(grad_scores, query, TN).astype(BF)
        moved_ref[2, :, cols] = mm(probs.astype(BF), outer, TN).astype(BF)
    back = jnp.zeros_like(grad)
    for s in range(3):
        back = back + mm(moved_ref[s, :, :span], own_qkv[s], NT)
        for d in range(1, groups):
            back = back + mm(moved_ref[s, :, d * span : (d + 1) * span], far_qkv[d - 1, s], NT)
    finish_back(grad, back, x_ref, gain_ref, new_refs, gain_out, bias_out)


def finish_back(grad, back, x_ref, gain_ref, new_refs, gain_out, bias_out):
    hat, scale = row_stats(x_ref[...])
    grad = grad + norm_pull(back, hat, scale, gain_ref[...])
    for new_ref in new_refs:
        new_ref[...] = grad.astype(new_ref.dtype)

    @pl.when(pl.program_id(0) == 0)
    def _():
        gain_out[...] = jnp.zeros_like(gain_out)
        bias_out[...] = jnp.zeros_like(bias_out)

    gain_out[...] += jnp.sum(back * hat, axis=0, keepdims=True)
    bias_out[...] += jnp.sum(back, axis=0, keepdims=True)


def dense_kernel(groups, place_ref, x_ref, gain_ref, bias_ref, *refs):
    many = 8 * groups - 6
    new_ref, normed_ref, act_ref, slope_ref = refs[many : many + 4]
    targets, sems = refs[many + 4 : -1], refs[-1]
    copies = dense_copies(place_ref[0], refs[:many], targets, sems)
    firsts = [targets[0]] + [targets[2].at[d] for d in range(groups - 1)]
    seconds = [targets[1]] + [targets[3].at[d] for d in range(groups - 1)]
    run_at_start(copies)
    values = x_ref[...]
    hat, _ = row_stats(values)
    normed = (hat * gain_ref[...] + bias_ref[...]).astype(BF)
    normed_ref[...] = normed
    wait_at_start(copies)
    span = targets[0].shape[-1]
    chunk = span // 2
    for d in range(groups):
        for part in range(2):
            inner = slice(part * chunk, (part + 1) * chunk)
            cols = slice(d * span + part * chunk, d * span + (part + 1) * chunk)
            act, slope = gelu_both(mm(normed, firsts[d][:, inner], NN))
            act = act.astype(BF)
            act_ref[:, cols] = act
            slope_ref[:, cols] = slope.astype(BF)
            values = values + mm(act, seconds[d][inner], NN)
    new_ref[...] = values


def dense_back_kernel(groups, place_ref, grad_ref, x_ref, slope_ref, gain_ref, *refs):
    many = 8 * groups - 6
    moved_ref, gain_out, bias_out = refs[many : many + 3]
    new_refs = refs[many + 3 : -5]
    targets, sems = refs[-5:-1], refs[-1]
    copies = dense_copies(place_ref[0], refs[:many], targets, sems)
    firsts = [targets[0]] + [targets[2].at[d] for d in range(groups - 1)]
    seconds = [targets[1]] + [targets[3].at[d] for d in range(groups - 1)]
    run_at_start(copies)
    grad = grad_ref[...]
    low = grad.astype(BF)
    wait_at_start(copies)
    span = targets[0].shape[-1]
    chunk = span // 2
    back = jnp.zeros_like(grad)
    for d in range(groups):
        for part in range(2):
            inner = slice(part * chunk, (part + 1) * chunk)
            cols = slice(d * span + part * chunk, d * span + (part + 1) * chunk)
            hidden = mm(low, seconds[d][inner], NT) * slope_ref[:, cols].astype(F32)
            hidden = hidden.astype(BF)
            moved_ref[:, cols] = hidden
            back = back + mm(hidden, firsts[d][:, inner], NT)
    finish_back(grad, back, x_ref, gain_ref, new_refs, gain_out, bias_out)


def image_block(*shape):
    lead = len(shape) - 2
    return pl.BlockSpec(shape, lambda i: (0,) * lead + (i, 0))


def fixed_block(*shape):
    return pl.BlockSpec(shape, lambda i: (0,) * len(shape))


RAW = pl.BlockSpec(memory_space=pl.ANY)


def dense_call(kernel, place, rows, singles, flat, outs, scratch, flops):
    buffers, copies = scratch
    specs = [pl.BlockSpec(memory_space=pltpu.SMEM)]
    specs += [image_block(*r.shape[:-2], ROWS, r.shape[-1]) for r in rows]
    specs += [fixed_block(*r.shape) for r in singles]
    specs += [RAW] * len(flat)
    out_specs = [
        image_block(*o.shape[:-2], ROWS, o.shape[-1]) if o.shape[-2] > 1 else fixed_block(*o.shape)
        for o in outs
    ]
    moved = sum(o.size * o.dtype.itemsize for o in list(outs) + list(rows) + flat)
    return pl.pallas_call(
        kernel,
        grid=(rows[0].shape[-2] // ROWS,),
        in_specs=specs,
        out_specs=out_specs,
        out_shape=outs,
        scratch_shapes=[pltpu.VMEM(b, BF) for b in buffers]
        + [pltpu.SemaphoreType.DMA((copies,))],
        cost_estimate=cost_of(flops, moved),
    )(place, *rows, *singles, *flat)


def cost_of(flops, moved):
    return pl.CostEstimate(
        flops=int(COST * flops), bytes_accessed=int(COST * moved), transcendentals=0
    )


def shape(*dims, kind=BF):
    return jax.ShapeDtypeStruct(dims, kind)


def attend_forward(layer, groups, place, values, gain, bias, weights, follow=()):
    rows, width = values.shape
    outs = (
        shape(rows, width, kind=F32),
        shape(rows, width),
        shape(3, rows, width),
        shape(rows, width),
        shape(rows, 128, kind=F32),
    ) + (shape(rows, width),) * bool(follow)
    return dense_call(
        functools.partial(attend_kernel, layer, groups, bool(follow)),
        place, (values,), (gain, bias) + follow, weights, outs, attend_scratch(width, groups),
        rows * width * (8 * width + 4 * ROWS),
    )


def attend_backward(
    layer, groups, place, grad, values, gain, packed, total, weights, kinds
):
    rows, width = values.shape
    outs = (
        shape(3, rows, width),
        shape(1, width, kind=F32),
        shape(1, width, kind=F32),
    ) + tuple(shape(rows, width, kind=k) for k in kinds)
    return dense_call(
        functools.partial(attend_back_kernel, layer, groups),
        place, (grad, values, packed, total), (gain,), weights, outs,
        attend_scratch(width, groups), rows * width * (8 * width + 10 * ROWS),
    )


def dense_forward(groups, place, values, gain, bias, weights):
    rows, width = values.shape
    hidden = groups * weights[0].shape[-1]
    outs = (
        shape(rows, width, kind=F32),
        shape(rows, width),
        shape(rows, hidden),
        shape(rows, hidden),
    )
    return dense_call(
        functools.partial(dense_kernel, groups),
        place, (values,), (gain, bias), weights, outs, dense_scratch(width, hidden, groups),
        4 * rows * width * hidden,
    )


def dense_backward(groups, place, grad, values, gain, slope, weights):
    rows, width = values.shape
    hidden = groups * weights[0].shape[-1]
    outs = (
        shape(rows, hidden),
        shape(1, width, kind=F32),
        shape(1, width, kind=F32),
        shape(rows, width, kind=F32),
        shape(rows, width),
    )
    return dense_call(
        functools.partial(dense_back_kernel, groups),
        place, (grad, values, slope), (gain,), weights, outs,
        dense_scratch(width, hidden, groups), 4 * rows * width * hidden,
    )


def expert_kernel(rows_ref, *refs):
    weights, (out_ref, act_ref, slope_ref) = refs[:-3], refs[-3:]
    rows = rows_ref[...]
    width = rows.shape[1]
    span = weights[0].shape[1]
    total = jnp.zeros(rows.shape, F32)
    for j, weight in enumerate(weights):
        cols = slice(j * span, (j + 1) * span)
        act, slope = gelu_both(mm(rows, weight[:width], NN))
        act = act.astype(BF)
        act_ref[:, cols] = act
        slope_ref[:, cols] = slope.astype(BF)
        parts = [mm(act, weight[k : k + span], NN) for k in range(width, 2 * width, span)]
        total = total + (jnp.concatenate(parts, 1) if len(parts) > 1 else parts[0])
    out_ref[...] = total.astype(BF)


def expert_back_kernel(grad_ref, slope_ref, *refs):
    weights, (out_ref, hidden_ref) = refs[:-2], refs[-2:]
    grad = grad_ref[...]
    width = grad.shape[1]
    span = weights[0].shape[1]
    total = jnp.zeros(grad.shape, F32)
    for j, weight in enumerate(weights):
        cols = slice(j * span, (j + 1) * span)
        parts = [
            mm(grad[:, k : k + span], weight[width + k : width + k + span], NT)
            for k in range(0, width, span)
        ]
        hidden = (sum(parts) * slope_ref[:, cols].astype(F32)).astype(BF)
        hidden_ref[:, cols] = hidden
        total = total + mm(hidden, weight[:width], NT)
    out_ref[...] = total.astype(BF)


def expert_call(kernel, rows, weights, outs):
    count = rows[0].shape[0]
    tile = 256 if count % 256 == 0 else 128
    hold = [
        pl.BlockSpec(w.shape, lambda i: (0, 0), pipeline_mode=pl.Buffered(1)) for w in weights
    ]
    moved = sum(o.size * o.dtype.itemsize for o in list(outs) + list(rows) + list(weights))
    return pl.pallas_call(
        kernel,
        grid=(count // tile,),
        in_specs=[image_spec(tile, r) for r in rows] + hold,
        out_specs=[image_spec(tile, o) for o in outs],
        out_shape=outs,
        cost_estimate=cost_of(2 * count * sum(w.size for w in weights), moved),
    )(*rows, *weights)


def image_spec(tile, like):
    return pl.BlockSpec((tile, like.shape[1]), lambda i: (i, 0))


def expert_forward(rows, weights):
    count, width = rows.shape
    hidden = len(weights) * weights[0].shape[1]
    outs = (shape(count, width), shape(count, hidden), shape(count, hidden))
    return expert_call(expert_kernel, (rows,), weights, outs)


def expert_backward(grad, slope, weights):
    outs = (shape(*grad.shape), shape(*slope.shape))
    return expert_call(expert_back_kernel, (grad, slope), weights, outs)


def weight_kernel(groups, lines, mover_ref, *refs):
    stats, refs = refs[:lines], refs[lines:]
    count = (len(refs) - 2) // 2
    lefts, rights, (keep_ref, send_ref) = refs[:count], refs[count:-2], refs[-2:]
    half = keep_ref.shape[0]
    turned = [mm(mover_ref[...], left[...], NT).astype(BF) for left in lefts]
    at = 0
    columns = keep_ref.shape[1] // groups
    for left, right in zip(turned, rights):
        for s in range(right.shape[0] if len(right.shape) == 3 else 1):
            source = right.at[s] if len(right.shape) == 3 else right
            span = source.shape[1] // groups
            tile = min(source.shape[1], 768)
            for k in range(0, source.shape[1], tile):
                part = mm(left, source[:, k : k + tile], NN).astype(BF)
                for j in range(k, k + tile, min(span, tile)):
                    low = (j // span) * columns + at + j % span
                    high = low + min(span, tile)
                    piece = part[:, j - k : j - k + min(span, tile)]
                    keep_ref[:, low:high] = piece[:half]
                    send_ref[:, low:high] = piece[half:]
            at += span
    if lines:
        rows = [stat[...] for stat in stats]
        room = columns - at
        rows.append(jnp.zeros((room - sum(r.shape[0] for r in rows), half * 2), F32))
        piece = mm(mover_ref[...], jnp.concatenate(rows, 0).astype(BF), NT).astype(BF)
        for d in range(groups):
            keep_ref[:, d * columns + at : (d + 1) * columns] = piece[:half]
            send_ref[:, d * columns + at : (d + 1) * columns] = piece[half:]


def weight_grads(groups, mover, pairs, stats=()):
    width = mover.shape[0]
    columns = sum(r.size // r.shape[-2] for _, r in pairs)
    columns += groups * -(-sum(r.shape[0] for r in stats) // 128) * 128
    out = shape(width // 2, columns)
    rows = pairs[0][0].shape[0]
    operands = [mover, *stats] + [p[0] for p in pairs] + [p[1] for p in pairs]
    return pl.pallas_call(
        functools.partial(weight_kernel, groups, len(stats)),
        in_specs=[pl.BlockSpec(memory_space=pltpu.VMEM)] * len(operands),
        out_specs=[pl.BlockSpec(memory_space=pltpu.VMEM)] * 2,
        out_shape=(out, out),
        cost_estimate=cost_of(
            2 * width * columns * rows, sum(2 * o.size for o in operands) + 4 * out.size
        ),
    )(*operands)


def dispatch_kernel(part, far, back, extra_ref, lines_ref, gates_ref, rows_ref, *refs):
    seats, got, refs = refs[:far], refs[far : 2 * far], refs[2 * far :]
    out_ref = refs[back]
    tile = out_ref.shape[0]
    base = pl.program_id(0) * tile
    ids = base + lax.broadcasted_iota(jnp.int32, (tile, lines_ref.shape[1]), 0)
    first, second = ids == lines_ref[:1], ids == lines_ref[1:]
    total = mm((first | second).astype(F32).astype(BF), rows_ref[...], NN)
    if back:
        gates = jnp.where(first, gates_ref[:1], 0.0) + jnp.where(second, gates_ref[1:], 0.0)
        refs[2][...] = jnp.sum(total * refs[0][...].astype(F32), axis=1, keepdims=True)
        total = total * jnp.sum(gates, axis=1, keepdims=True)
    else:
        line = base + lax.broadcasted_iota(jnp.int32, (tile, 1), 0)
        total = total + jnp.where(line % part == part - 1, extra_ref[0], 0.0)
    for seat, x in zip(seats, got):
        ids = base + lax.broadcasted_iota(jnp.int32, (tile, seat.shape[1]), 0)
        total = total + mm((ids == seat[...]).astype(F32).astype(BF), x[...], NN)
    out_ref[...] = total.astype(BF)


def dispatch_call(part, slots, extra, lines, gates, rows, seats, got, merged=None):
    tile = 256 if slots % 256 == 0 else 128
    width = rows.shape[1]
    back = merged is not None
    held = [lines, gates, rows, *seats, *got]
    block = pl.BlockSpec((tile, width), lambda i: (i, 0))
    outs = (shape(slots, width),)
    specs = (block,)
    if back:
        outs += (shape(slots, 1, kind=F32),)
        specs += (pl.BlockSpec((tile, 1), lambda i: (i, 0)),)
    inputs = held + [merged] * back
    return pl.pallas_call(
        functools.partial(dispatch_kernel, part, len(got), back),
        grid=(slots // tile,),
        in_specs=[pl.BlockSpec(memory_space=pltpu.SMEM)]
        + [fixed_block(*x.shape) for x in held]
        + [block] * back,
        out_specs=specs,
        out_shape=outs,
        cost_estimate=cost_of(2 * slots * rows.size, 2 * (slots * width + rows.size)),
    )(extra, *inputs)


def picks_of(pack, number, weighted, count):
    ids = lax.broadcasted_iota(jnp.int32, (pack.shape[0], count), 1)
    cols = pack[:, 3 + 2 * number : 5 + 2 * number].astype(jnp.int32)
    first, second = ids == cols[:, :1], ids == cols[:, 1:]
    if not weighted:
        return (first | second).astype(F32).astype(BF)
    return (jnp.where(first, pack[:, :1], 0.0) + jnp.where(second, pack[:, 1:2], 0.0)).astype(BF)


def combine_kernel(pack_ref, x_ref, teacher_ref, *refs):
    rows, (final_ref, grad_ref, low_ref) = refs[:-3], refs[-3:]
    total, pack = x_ref[...], pack_ref[...]
    for number, source in enumerate(rows):
        total = total + mm(picks_of(pack, number, True, source.shape[0]), source[...], NN)
    final_ref[...] = total.astype(BF)
    grad = pack[:, 2:3] * (total - teacher_ref[...].astype(F32))
    grad_ref[...] = grad
    low_ref[...] = grad.astype(BF)


def combine_back_kernel(far, pack_ref, x_ref, grad_ref, logits_ref, *refs):
    rows, refs = refs[: far + 1], refs[far + 1 :]
    router_ref, gain_ref, gain_out, bias_out, *new_refs = refs
    total, pack = mm(logits_ref[...], router_ref[...], NT), pack_ref[...]
    for number, source in enumerate(rows):
        total = total + mm(picks_of(pack, number, False, source.shape[0]), source[...], NN)
    finish_back(grad_ref[...], total, x_ref, gain_ref, new_refs, gain_out, bias_out)


def combine_call(kernel, tiled, held, outs):
    moved = sum(x.size * x.dtype.itemsize for x in list(tiled) + list(held) + list(outs))
    return pl.pallas_call(
        kernel,
        grid=(tiled[0].shape[0] // ROWS,),
        in_specs=[image_block(ROWS, x.shape[1]) for x in tiled]
        + [fixed_block(*x.shape) for x in held],
        out_specs=[
            image_block(ROWS, o.shape[1]) if o.shape[0] > 1 else fixed_block(*o.shape) for o in outs
        ],
        out_shape=outs,
        cost_estimate=cost_of(2 * tiled[0].shape[0] * held[0].size, moved),
    )(*tiled, *held)


def outer_kernel(left_ref, right_ref, *refs):
    part = mm(left_ref[...], right_ref[...], TN)
    for got in refs[:-1]:
        part = part + got[...].astype(F32)
    refs[-1][...] = part.astype(refs[-1].dtype)


def expert_grads(left, right, width, span, odd, got=None, cut_left=True):
    rows = left.shape[0]
    wide = left.shape[1] if cut_left else right.shape[1]
    count = wide // (2 * span)
    high, low = (span, width) if cut_left else (width, span)
    cut = pl.BlockSpec((rows, span), lambda j: (0, 2 * j + odd))
    whole = pl.BlockSpec((rows, width), lambda j: (0, 0))
    block = pl.BlockSpec((high, low), lambda j: (j, 0))
    more = () if got is None else (got,)
    out = shape(count * high, low)
    return pl.pallas_call(
        outer_kernel,
        grid=(count,),
        in_specs=([cut, whole] if cut_left else [whole, cut]) + [block] * len(more),
        out_specs=block,
        out_shape=out,
        cost_estimate=cost_of(2 * out.size * rows, 2 * (left.size + right.size + 2 * out.size)),
    )(left, right, *more)


def pinned_all(values, *others):
    return lax.optimization_barrier(tuple(values) + others)[: len(values)]


def pinned(value, *others):
    return lax.optimization_barrier((value,) + others)[0]


def body(
    tokens,
    teacher,
    valid_flags,
    routes,
    capacity,
    norm_gains,
    norm_biases,
    attn_qkv,
    attn_out,
    mlp_in,
    mlp_out,
    router,
    expert_in,
    expert_out,
):
    owners = lax.axis_size("expert")
    groups = lax.axis_size("tensor")
    place = lax.axis_index("expert")
    group = lax.axis_index("tensor")
    local_rows, width = tokens.shape
    experts = router.shape[1]
    image_count = local_rows // SEQ
    images = -(-image_count // groups)
    own_rows = images * ROWS
    all_rows = groups * own_rows
    capacity_most = 4 * (3 * local_rows // (4 * experts))
    used = -(-capacity_most // (2 * groups))
    part = -(-(used + 1) // 16) * 16
    slots = owners * part
    gains = norm_gains.astype(F32)
    biases = norm_biases.astype(F32)

    def relative(rows, fill, count):
        shape = rows.shape[1:]
        grid = rows.reshape((image_count, SEQ) + shape)
        grid = jnp.pad(
            grid,
            [(0, groups * images - image_count), (0, ROWS - SEQ)] + [(0, 0)] * len(shape),
            constant_values=fill,
        )
        taken = [
            lax.dynamic_slice_in_dim(grid, (group ^ d) * images, images, 0) for d in range(count)
        ]
        return jnp.concatenate(taken, 0).reshape((count * own_rows,) + shape)

    def absolute(rows):
        shape = rows.shape[1:]
        grid = rows.reshape((groups * images, ROWS) + shape)
        taken = [
            lax.dynamic_slice_in_dim(grid, (group ^ d) * images, images, 0) for d in range(groups)
        ]
        grid = jnp.concatenate(taken, 0)[:image_count, :SEQ]
        return grid.reshape((local_rows,) + shape)

    place_ref = jnp.full((1,), place, jnp.int32)
    gain_rows = [gains[j : j + 1] for j in range(4)]
    bias_rows = [biases[j : j + 1] for j in range(4)]

    quarter = place % 4

    def attend_piece(layer):
        span = attn_out.shape[1]
        rows, few = width // 4, span // 4
        qkv_part = lax.dynamic_slice(
            attn_qkv, (layer, 0, quarter * rows, 0), (1, 3, rows, span)
        ).reshape(3 * rows, span)
        out_part = lax.dynamic_slice(attn_out, (layer, quarter * few, 0), (1, few, width))[0]
        parts = [out_part[:, j * span : (j + 1) * span] for j in range(groups)]
        return jnp.concatenate([qkv_part] + parts, 0)

    def rows_of(weight, number):
        rows = weight.shape[0] // 4
        return lax.dynamic_slice_in_dim(weight, number * rows, rows, 0)

    def over_tensor(value):
        return [swap(value, "tensor", d) for d in range(1, groups)]

    def both_cores(value):
        return [value, swap(value, "expert", 1)]

    last = [None]

    def after(*values):
        if last[0] is not None:
            values = pinned_all(values, last[0])
        return values if len(values) > 1 else values[0]

    def mark(value):
        last[0] = value
        return value

    def leg(parts, distance):
        return [swap(part, "expert", distance) for part in parts]

    def joined(first, second, third, last):
        return [x for four in zip(first, third, second, last) for x in four]

    piece_first = mark(attend_piece(0))
    first_x = over_tensor(piece_first)
    piece_in = mark(rows_of(after(mlp_in), quarter))
    piece_out = mark(rows_of(after(mlp_out), place % 2 + place // 4 % 2 * 2))
    piece_second = mark(attend_piece(1))
    tokens = after(tokens)
    start = mark(relative(tokens, 0, 1).astype(F32))
    first_x = [after(x) for x in first_x]
    in_x, out_x = over_tensor(piece_in), over_tensor(piece_out)
    second_x = over_tensor(piece_second)
    first_y, first_c = leg(first_x, 2), leg(first_x, 1)
    first_l = leg(first_y, 1)
    weights_first = [attn_qkv, attn_out] + joined(first_x, first_y, first_c, first_l)

    room = 2 * used
    kind = jnp.int32
    routes = pinned(routes, first_x[0])
    expert_of = jnp.concatenate([routes[:, 0], routes[:, 1]])
    owner = jnp.tile(jnp.arange(local_rows, dtype=kind) // (SEQ * images), 2)
    of_expert = (expert_of[:, None] == jnp.arange(experts, dtype=kind)).astype(kind)
    of_owner = (owner[:, None] == jnp.arange(groups, dtype=kind)).astype(kind)
    both = (
        (expert_of * groups + owner)[:, None] == jnp.arange(experts * groups, dtype=kind)
    ).astype(kind)
    earlier = (jnp.cumsum(both, axis=0) - both).reshape(-1, experts, groups)
    ahead = jnp.sum(earlier * of_expert[:, :, None], axis=1)
    rank = jnp.sum(ahead * of_owner, axis=1)
    kept_mask = jnp.sum(ahead, axis=1) < jnp.sum(of_expert * capacity[None, :], axis=1)
    held = jnp.sum(both * kept_mask[:, None].astype(kind), axis=0).reshape(experts, groups)
    inside = jnp.minimum(held, room)
    beyond = held - inside
    free = room - inside

    def before(counts):
        return jnp.cumsum(counts, axis=1) - counts

    def of_pair(table):
        return jnp.sum(of_expert[:, :, None] * table[None], axis=1)

    late = jnp.sum(of_pair(before(beyond)) * of_owner, axis=1) + rank - room
    free_from = of_pair(before(free))
    hit = (late[:, None] >= free_from) & (late[:, None] < free_from + of_pair(free))
    hit = hit.astype(kind)
    fits = rank < room
    at = jnp.where(fits, rank, jnp.sum(hit * (of_pair(inside) + late[:, None] - free_from), axis=1))
    home = jnp.where(fits, owner, jnp.sum(hit * jnp.arange(groups, dtype=kind), axis=1))
    row_of = (2 * expert_of + at // used) * part + at % used

    def own_pairs(values):
        return relative(values.reshape(2, local_rows).T, -1, 1)

    local_row = own_pairs(jnp.where(kept_mask & (owner == group) & (home == group), row_of, -1))
    most = min(experts, 2 * SEQ * images // capacity_most)
    rest = min(2 * SEQ * images - most * capacity_most, capacity_most) - room
    most = most * (capacity_most - room) + max(rest, 0)
    most = -(-most // 16) * 16
    few = min(64, most)
    masks = []
    for d in range(1, groups):
        masks.append(kept_mask & (owner == group) & (home == group ^ d))
        masks.append(kept_mask & (owner == group ^ d) & (home == group))
    masks = jnp.stack(masks, 1).astype(kind)
    ranks = jnp.cumsum(masks, axis=0) - masks
    ranks = jnp.where(masks > 0, ranks, -1)
    guest_out, guest_in = [], []
    for d in range(1, groups):
        guest_out.append(own_pairs(ranks[:, 2 * d - 2]))
        named = ranks[:, 2 * d - 1][None, :] == jnp.arange(most, dtype=kind)[:, None]
        guest_in.append(jnp.sum(jnp.where(named, row_of[None, :] + 1, 0), axis=1) - 1)
    distances = [1 << k for k in range(owners.bit_length() - 1)]

    def wider(value, step, *others):
        got = swap(value, "expert", step)
        return jnp.maximum(value, pinned(got, *others) if others else got)

    crowd = wider(jnp.full((8, 128), jnp.max(beyond.sum(0)), kind), 1)
    routes_own = relative(routes, 0, 1)
    valid_rows = relative(jnp.repeat(valid_flags.astype(F32), SEQ)[:, None], 0, 1)

    in_x = pinned_all(in_x, *first_l)
    start = pinned(start, *in_x, local_row, crowd)
    after_attn, normed_first, packed_first, mixed_first, total_first = attend_forward(
        0, groups, place_ref, start, gain_rows[0], bias_rows[0], weights_first
    )
    crowd = wider(crowd, 4, after_attn)
    out_x = pinned_all(out_x, after_attn)
    second_x = pinned_all(second_x, *out_x)
    in_y, in_c = leg(in_x, 2), leg(in_x, 1)
    out_y, out_c = leg(out_x, 4), leg(out_x, 1)
    in_y, out_y = pinned_all(in_y, after_attn), pinned_all(out_y, *second_x)
    crowd = wider(crowd, 8, *out_y)
    weights_dense = [mlp_in, mlp_out] + joined(in_x, in_y, in_c, leg(in_y, 1))
    weights_dense += joined(out_x, out_y, out_c, leg(out_y, 1))
    second_y, second_c = leg(second_x, 2), leg(second_x, 1)
    after_dense, normed_dense, dense_act, dense_slope = dense_forward(
        groups, place_ref, pinned(after_attn, crowd, *second_x), gain_rows[1], bias_rows[1],
        weights_dense,
    )
    second_y = pinned_all(second_y, after_dense)
    weights_second = [attn_qkv, attn_out] + joined(second_x, second_y, second_c, leg(second_y, 1))
    second = attend_forward(
        1, groups, place_ref, pinned(after_dense, crowd), gain_rows[2], bias_rows[2],
        weights_second, (gain_rows[3], bias_rows[3]),
    )
    after_second, normed_second, packed_second, mixed_second, total_second, normed_expert = second
    for step in [2] + distances[4:]:
        crowd = wider(crowd, step, after_second)
    logits = mm(normed_expert, router, NN)
    picker = routes_own[:, :, None] == jnp.arange(experts, dtype=kind)[None, None, :]
    chosen = jnp.sum(jnp.where(picker, logits[:, None, :], 0.0), axis=2)
    gate_vals = jax.nn.softmax(chosen, axis=1)
    gate_lines = gate_vals.T
    local_lines = local_row.T
    slot_ids = jnp.arange(slots, dtype=kind)

    def guests(count):
        ids = jnp.arange(count, dtype=kind)[:, None]
        return [(ids == g[None, :, 0], ids == g[None, :, 1]) for g in guest_out]

    def chosen_rows(count, rows):
        return [mm((a | b).astype(BF), rows, NN) for a, b in guests(count)]

    def returned_rows(count, rows):
        return [
            mm((g[:count, None] == slot_ids[None, :]).astype(BF), rows, NN).astype(BF)
            for g in guest_in
        ]

    def seats(count):
        return [g[None, :count] for g in guest_in]

    def over(rows):
        return [swap(x, "tensor", d + 1) for d, x in enumerate(rows)]

    def sized(branch, *operands):
        if few == most:
            return branch(few)(*operands)
        return lax.cond(crowd[0, 0] <= few, branch(few), branch(most), *operands)

    def grown(rows):
        return jnp.pad(rows, ((0, most - rows.shape[0]), (0, 0)))

    def across(rows):
        return lax.all_to_all(
            rows.reshape(owners, part, width), "expert", split_axis=0, concat_axis=0, tiled=True
        ).reshape(slots, width)

    images_valid = jnp.sum(valid_flags.astype(F32)).reshape(1)
    blank = jnp.zeros((2, own_rows), F32)

    def dispatch(count):
        def branch(rows):
            got = over([x.astype(BF) for x in chosen_rows(count, rows)])
            return dispatch_call(
                part, slots, images_valid, local_lines, blank, rows, seats(count), got
            )[0]

        return branch

    sent_rows = sized(dispatch, normed_expert)
    span = expert_in.shape[2]
    blocks = [expert_out[0, :, k : k + span] for k in range(0, width, span)]
    expert_own = pinned(jnp.concatenate([expert_in[0]] + blocks, 0), sent_rows)
    expert_parts = [x for w in [expert_own] + over_tensor(expert_own) for x in both_cores(w)]
    rows_in = across(sent_rows)
    valid_count = SEQ * jnp.sum(rows_in[part - 1 :: part, :1].astype(F32))
    teacher_rel = relative(teacher, 0, 1)
    scale = (local_rows * owners / valid_count) * valid_rows
    rows_in = pinned(rows_in, teacher_rel, scale)
    expert_rows, act, slope = expert_forward(rows_in, expert_parts)
    pairs = [x.astype(F32) for x in (local_row, *guest_out)]
    pack = jnp.concatenate([gate_vals, scale] + pairs, 1)
    pack = jnp.pad(pack, ((0, 0), (0, 128 - pack.shape[1])))
    merged = across(expert_rows)
    merged, pack = pinned_all((merged, pack), expert_rows)

    outs = (shape(own_rows, width), shape(own_rows, width, kind=F32), shape(own_rows, width))

    def combine(count):
        def branch(rows):
            got = over(returned_rows(count, rows))
            results = combine_call(
                combine_kernel, (pack, after_second, teacher_rel), (rows, *got), outs
            )
            return tuple(results) + tuple(grown(x) for x in got)

        return branch

    final_low, grad_final, grad_low, *lodged = sized(combine, merged)

    def dispatch_back(count):
        def branch(rows, merged, *lodged):
            sent, parts = [], []
            for (a, b), x, taken in zip(guests(count), lodged, chosen_rows(count, rows)):
                gates = jnp.sum(
                    jnp.where(a, gate_lines[:1], 0.0) + jnp.where(b, gate_lines[1:], 0.0),
                    axis=1,
                    keepdims=True,
                )
                sent.append((gates * taken).astype(BF))
                inner = jnp.sum(taken * x[:count].astype(F32), axis=1, keepdims=True)
                parts.append(grown(inner))
            results = dispatch_call(
                part, slots, images_valid, local_lines, gate_lines, rows, seats(count),
                over(sent), merged,
            )
            return tuple(results) + tuple(parts)

        return branch

    sent_back, grad_slot_gate, *grad_guest_gate = sized(
        dispatch_back, grad_low, merged, *lodged
    )
    final_far = over_tensor(pinned(final_low, sent_back))
    grad_out_rows = across(sent_back)
    grad_rows, grad_hidden = expert_backward(
        pinned(grad_out_rows, *final_far), slope, expert_parts
    )
    activations = absolute(jnp.concatenate([final_low] + list(pinned_all(final_far, grad_rows)), 0))
    grad_back = across(grad_rows)

    def start_groups(total):
        span = total.shape[1] // groups
        sent = [total[:, d * span : (d + 1) * span].astype(BF) for d in range(1, groups)]
        return total[:, :span], sent

    def start_rows(total):
        rows = total.shape[0] // 2
        return total[:rows], [total[rows:].astype(BF)]

    def cross(sent):
        return [swap(x, "tensor", d + 1) for d, x in enumerate(sent)]

    def along(sent, distance):
        return [swap(x, "expert", distance) for x in sent]

    def finish(keep, got, *after):
        total = keep.astype(F32)
        for x in got:
            total = total + (pinned(x, *after) if after else x).astype(F32)
        return total

    act, rows_in, grad_slot_gate = pinned_all((act, rows_in, grad_slot_gate), grad_rows)
    grad_own = []
    for choice in range(2):
        taken = slot_ids[:, None] == local_row[None, :, choice]
        total = jnp.sum(jnp.where(taken, grad_slot_gate, 0.0), axis=0)
        for pair, values in zip(guests(most), grad_guest_gate):
            total = total + jnp.sum(jnp.where(pair[choice], values, 0.0), axis=0)
        grad_own.append(total)
    grad_own = jnp.stack(grad_own, 1)
    span = expert_in.shape[2]
    sent = mark(expert_grads(act, grad_out_rows, width, span, 1))
    got_eo = along([sent], 1)[0]
    sent = mark(expert_grads(after(rows_in), grad_hidden, width, span, 1, None, False))
    got_ei = along([sent], 1)[0]

    def shares_of(total, rows):
        return total[:rows], [total[d * rows : (d + 1) * rows] for d in range(1, groups)]

    keep_eo, sent_eo = shares_of(
        mark(expert_grads(act, grad_out_rows, width, span, 0, after(got_eo))), span
    )
    got_eo = cross(sent_eo)
    keep_ei, sent_ei = shares_of(
        mark(expert_grads(rows_in, grad_hidden, width, span, 0, after(got_ei), False)), width
    )

    own_gates = gate_vals
    grad_chosen = own_gates * (grad_own - jnp.sum(own_gates * grad_own, axis=1, keepdims=True))
    grad_logits = jnp.sum(
        jnp.where(picker, grad_chosen[:, :, None], 0.0), axis=1
    ).astype(BF)
    grad_router = mm(grad_logits, normed_expert, TN)
    grad_back = pinned(grad_back, *sent_ei, *got_eo, grad_router, activations)

    outs = (shape(1, width, kind=F32),) * 2 + (
        shape(own_rows, width, kind=F32), shape(own_rows, width),
    )

    def combine_back(count):
        def branch(rows):
            results = combine_call(
                functools.partial(combine_back_kernel, groups - 1),
                (pack, after_second, grad_final, grad_logits),
                (rows, *over(returned_rows(count, rows)), router, gain_rows[3]),
                outs,
            )
            return tuple(results)

        return branch

    gain_four, bias_four, grad_second, low_second = sized(combine_back, grad_back)
    got_ei = cross([pinned(p, grad_second) for p in sent_ei])

    block = width // owners
    feature = jnp.arange(width, dtype=jnp.int32)

    def mover_of(distances):
        ahead, turned = feature // block, 0
        for distance in reversed(distances):
            turned = turned + distance * (ahead % 2)
            ahead = ahead // 2
        source = (turned ^ place) * block + feature % block
        return (source[:, None] == feature[None, :]).astype(BF)

    mover = mover_of(distances)
    turned_order = [1, 4, 2] + distances[3:]
    mover_turned = mover_of(turned_order)

    mark(grad_second)
    def arrive(keep, got):
        return finish(keep, [after(x) for x in got])

    grads_second, gain_three, bias_three, grad_dense, low_dense = attend_backward(
        1, groups, place_ref, grad_second, after_dense, gain_rows[2], packed_second,
        total_second, weights_second, (F32, BF),
    )
    mark(grad_dense)
    got_ei = [after(x) for x in got_ei]
    keep_a, send_a = weight_grads(
        groups,
        mover,
        [(pinned(normed_second, *got_ei), grads_second), (low_second, mixed_second)],
    )
    mark(send_a)
    got_a = along([send_a], 1)
    low_dense = after(low_dense)
    keep_b, send_b = weight_grads(groups, mover, [(low_dense, dense_act)])
    mark(send_b)
    got_b = along([send_b], 1)
    keep_a, sent_a = start_groups(arrive(keep_a, got_a).astype(BF))
    mark(sent_a[0])
    got_a = cross(sent_a)
    grad_hidden, gain_two, bias_two, grad_attn, low_first = dense_backward(
        groups, place_ref, after(grad_dense), after_attn, gain_rows[1], dense_slope, weights_dense,
    )
    mark(grad_attn)
    keep_b, sent_b = start_rows(arrive(keep_b, got_b).astype(BF))
    mark(sent_b[0])
    got_b = along(sent_b, 2)

    got_a = [after(x) for x in got_a]
    stats = [gain_two, gain_three, gain_four, bias_two, bias_three, bias_four]
    keep_c, send_c = weight_grads(
        groups,
        mover_turned,
        [
            (pinned(normed_dense, *got_a), grad_hidden),
            (low_first, mixed_first),
        ],
        stats + [grad_router],
    )
    mark(send_c)
    got_c = along([send_c], 1)
    keep_a, sent_a = start_rows(arrive(keep_a, got_a).astype(BF))
    mark(sent_a[0])
    got_a = along(sent_a, 2)
    keep_c, sent_c = start_rows(arrive(keep_c, got_c).astype(BF))
    mark(sent_c[0])
    got_c = along(sent_c, 4)
    grads_first, gain_one, bias_one, grad_start = attend_backward(
        0, groups, place_ref, after(grad_attn), start, gain_rows[0], packed_first, total_first,
        weights_first, (BF,),
    )
    mark(grad_start)
    start_far = over_tensor(grad_start)
    got_b = [after(x) for x in got_b]
    keep_d, send_d = weight_grads(
        groups,
        mover,
        [(pinned(normed_first, *got_b), grads_first)],
        [gain_one, bias_one],
    )
    mark(send_d)
    got_d = along([send_d], 1)
    keep_b, sent_b = start_groups(arrive(keep_b, got_b).astype(BF))
    mark(sent_b[0])
    got_b = cross(sent_b)
    keep_a, sent_a = start_rows(arrive(keep_a, got_a))
    mark(sent_a[0])
    got_a = along(sent_a, 4)
    total_c = mark(arrive(keep_c, got_c).astype(BF))
    total_d = arrive(keep_d, got_d).astype(BF)
    span = total_d.shape[1] // groups
    cut = attn_out.shape[1]
    far_d = [
        jnp.concatenate([total_d[:, d * span : d * span + cut] for d in range(groups)], 1),
        jnp.concatenate([total_d[:, d * span + cut : (d + 1) * span] for d in range(groups)], 1),
    ]
    keep_d, sent_d = start_groups(far_d[0])
    keep_e, sent_e = start_rows(far_d[1])
    mark(sent_e[0])
    got_d = cross(sent_d)
    got_e = along(sent_e, 2)
    keep_c, sent_c = start_rows(after(total_c))
    mark(sent_c[0])
    got_c = along(sent_c, 2)
    start_far = [after(x) for x in start_far]
    input_grad = mark(absolute(jnp.concatenate([grad_start] + start_far, 0)))
    keep_a, sent_a = start_rows(arrive(keep_a, got_a))
    mark(sent_a[0])
    got_a = along(sent_a, 8)
    keep_b, sent_b = start_rows(arrive(keep_b, got_b))
    mark(sent_b[0])
    got_b = along(sent_b, 4)
    keep_d, sent_d = start_rows(arrive(keep_d, got_d))
    mark(sent_d[0])
    got_d = along(sent_d, 2)
    keep_e, sent_e = start_groups(arrive(keep_e, got_e))
    mark(sent_e[0])
    got_e = cross(sent_e)
    keep_c, sent_c = start_groups(arrive(keep_c, got_c))
    mark(sent_c[0])
    got_c = cross(sent_c)
    total_a = mark(arrive(keep_a, got_a))
    keep_b, sent_b = start_rows(arrive(keep_b, got_b))
    mark(sent_b[0])
    got_b = along(sent_b, 8)
    total_d = arrive(keep_d, got_d)
    total_e = arrive(keep_e, got_e)
    keep_d, sent_d = start_rows(jnp.concatenate([total_d, total_e], 1))
    mark(sent_d[0])
    got_d = along(sent_d, 4)
    keep_c, sent_c = start_rows(arrive(keep_c, got_c))
    mark(sent_c[0])
    got_c = along(sent_c, 8)
    total_b = mark(arrive(keep_b, got_b))
    keep_d, sent_d = start_rows(arrive(keep_d, got_d))
    mark(sent_d[0])
    got_d = along(sent_d, 8)
    keep_eo, keep_ei = pinned_all((keep_eo, keep_ei), sent_d[0])
    grad_expert_out, grad_expert_in = finish(keep_eo, got_eo), finish(keep_ei, got_ei)
    total_c = arrive(keep_c, got_c)
    total_d = arrive(keep_d, [pinned(x, grad_expert_out, grad_expert_in, total_c) for x in got_d])
    joint = jnp.concatenate([total_a, total_b, total_c, total_d], 1)
    step = 16
    while step < owners:
        keep, sent = start_rows(joint)
        joint = finish(keep, along(sent, step))
        step *= 2
    spans = [attn_out.shape[1], mlp_in.shape[1], -(-(6 + experts) // 128) * 128]
    widths = [4 * spans[0], spans[1], spans[1], spans[0], spans[2], 3 * spans[0], 128]
    taken, at = [], 0
    for span in widths:
        taken.append(joint[:, at : at + span])
        at += span
    two, grad_mlp_out, grad_mlp_in = taken[0], taken[1].T, taken[2]
    one = jnp.concatenate([taken[5], taken[3]], 1)
    lines, last_lines = taken[4], taken[6]
    joint_small = jnp.concatenate(
        [last_lines[:, :1], lines[:, :3], last_lines[:, 1:2], lines[:, 3 : 6 + experts]], 1
    )

    def split_attention(total):
        span = total.shape[1] // 4
        return jnp.stack([total[:, s * span : (s + 1) * span] for s in range(3)]), total[:, -span:].T

    qkv_one, out_one = split_attention(one)
    qkv_two, out_two = split_attention(two)
    small = joint_small.T
    return (
        activations,
        input_grad,
        small[:4],
        small[4:7],
        small[7],
        jnp.stack([qkv_one, qkv_two]),
        jnp.stack([out_one, out_two]),
        grad_mlp_in,
        grad_mlp_out,
        small[8:].T,
        grad_expert_in[None],
        grad_expert_out[None],
    )


def solution(mesh):
    in_specs = (
        P("expert", None),
        P("expert", None),
        P("expert"),
        P("expert", None),
        P(),
        P(),
        P(),
        P(None, None, None, "tensor"),
        P(None, "tensor", None),
        P(None, "tensor"),
        P("tensor", None),
        P(),
        P("expert", None, "tensor"),
        P("expert", "tensor", None),
    )
    out_specs = (
        P("expert", None),
        P("expert", None),
        P(None, "expert"),
        P(None, "expert"),
        P("expert"),
        P(None, None, "expert", "tensor"),
        P(None, "tensor", "expert"),
        P("expert", "tensor"),
        P("tensor", "expert"),
        P("expert", None),
        P("expert", None, "tensor"),
        P("expert", "tensor", None),
    )
    return jax.shard_map(body, mesh=mesh, in_specs=in_specs, out_specs=out_specs, check_vma=False)
```

```python
import functools

import jax
import jax.numpy as jnp
from jax import lax
from jax.experimental import pallas as pl
from jax.experimental.pallas import tpu as pltpu
from jax.sharding import PartitionSpec as P

HD = 64
SEQ = 197
ROWS = 208
EPS = 1e-06
COST = 0.2
BF = jnp.bfloat16
F32 = jnp.float32


def mm(a, b, dims):
    return lax.dot_general(a, b, (dims, ((), ())), preferred_element_type=F32)


NN = ((1,), (0,))
NT = ((1,), (1,))
TN = ((0,), (0,))


def swap(value, axis, distance):
    size = lax.axis_size(axis)
    return lax.ppermute(value, axis, [(k, k ^ distance) for k in range(size)])


def gelu_both(x):
    k = 0.7978845608028654
    a = 0.044715 * k
    square = x * x
    half = 0.5 * jnp.tanh(x * (a * square + k)) + 0.5
    act = x * half
    return act, half + act * (1.0 - half) * (6.0 * a * square + 2.0 * k)


def row_stats(values):
    center = values - jnp.mean(values, axis=-1, keepdims=True)
    scale = lax.rsqrt(jnp.mean(center * center, axis=-1, keepdims=True) + EPS)
    return center * scale, scale


def norm_pull(grad, hat, scale, gain):
    inner = grad * gain
    first = jnp.mean(inner, axis=-1, keepdims=True)
    second = jnp.mean(inner * hat, axis=-1, keepdims=True)
    return scale * (inner - first - hat * second)


def attend_copies(layer, place, refs, targets, sems):
    qkv_in, out_in, parts = refs[0], refs[1], refs[2:]
    own_qkv, own_out, far_qkv, far_out = targets
    pairs = [(qkv_in.at[layer], own_qkv), (out_in.at[layer], own_out)]
    blocks, span = far_out.shape[1], far_out.shape[2]
    rows, few = far_qkv.shape[2] // 4, span // 4
    for k, part in enumerate(parts):
        d = k // 4
        quarter = (place % 4) ^ (k % 4)
        at = pl.multiple_of(quarter * rows, 16)
        for s in range(3):
            pairs.append((part.at[pl.ds(s * rows, rows)], far_qkv.at[d, s, pl.ds(at, rows)]))
        at = pl.multiple_of(quarter * few, 16)
        for j in range(blocks):
            source = part.at[pl.ds(3 * rows + j * few, few)]
            pairs.append((source, far_out.at[d, j, pl.ds(at, few)]))
    return [pltpu.make_async_copy(x, y, sems.at[n]) for n, (x, y) in enumerate(pairs)]


def dense_copies(place, refs, targets, sems):
    first_in, second_in, parts = refs[0], refs[1], refs[2:]
    own_first, own_second, far_first, far_second = targets
    pairs = [(first_in, own_first), (second_in, own_second)]
    quarters = (place % 4, place % 2 + place // 4 % 2 * 2)
    count = len(parts) // 2
    for k in range(count):
        for side, target in enumerate((far_first, far_second)):
            rows = target.shape[1] // 4
            at = pl.multiple_of((quarters[side] ^ (k % 4)) * rows, 16)
            pairs.append((parts[side * count + k], target.at[k // 4, pl.ds(at, rows)]))
    return [pltpu.make_async_copy(x, y, sems.at[n]) for n, (x, y) in enumerate(pairs)]


def attend_scratch(width, groups):
    span = width // groups
    return (
        (3, width, span), (span, width), (groups - 1, 3, width, span),
        (groups - 1, groups, span, span),
    ), 2 + 4 * (groups - 1) * (3 + groups)


def dense_scratch(width, hidden, groups):
    span = hidden // groups
    return (
        (width, span), (span, width), (groups - 1, width, span), (groups - 1, span, width),
    ), 2 + 8 * (groups - 1)


def run_at_start(copies):
    @pl.when(pl.program_id(0) == 0)
    def _():
        for copy in copies:
            copy.start()


def wait_at_start(copies):
    @pl.when(pl.program_id(0) == 0)
    def _():
        for copy in copies:
            copy.wait()


def pair_masks():
    left = lax.broadcasted_iota(jnp.int32, (ROWS, 2 * HD), 1) < HD
    seen = lax.broadcasted_iota(jnp.int32, (2 * ROWS, ROWS), 1) < SEQ
    return left, seen


def stack_pair(rows, left):
    none = jnp.zeros_like(rows)
    return jnp.concatenate([jnp.where(left, rows, none), jnp.where(left, none, rows)], 0)


def attend_kernel(layer, groups, follow, place_ref, x_ref, gain_ref, bias_ref, *refs):
    next_norm, refs = refs[: 2 * follow], refs[2 * follow :]
    many = 4 * groups - 2
    new_ref, normed_ref, packed_ref, mixed_ref, total_ref = refs[many : many + 5]
    targets, sems = refs[-5:-1], refs[-1]
    next_refs = refs[many + 5 : -5]
    own_qkv, own_out, far_qkv, far_out = targets
    copies = attend_copies(layer, place_ref[0], refs[:many], targets, sems)
    run_at_start(copies)
    values = x_ref[...]
    hat, _ = row_stats(values)
    normed = (hat * gain_ref[...] + bias_ref[...]).astype(BF)
    normed_ref[...] = normed
    wait_at_start(copies)
    span = own_qkv.shape[-1]
    for s in range(3):
        packed_ref[s, :, :span] = mm(normed, own_qkv[s], NN).astype(BF)
        for d in range(1, groups):
            part = mm(normed, far_qkv[d - 1, s], NN).astype(BF)
            packed_ref[s, :, d * span : (d + 1) * span] = part
    left, seen = pair_masks()
    lane = lax.broadcasted_iota(jnp.int32, (ROWS, 128), 1)
    totals = jnp.zeros((ROWS, 128), F32)
    for pair in range(packed_ref.shape[-1] // (2 * HD)):
        cols = slice(pair * 2 * HD, (pair + 1) * 2 * HD)
        query = stack_pair(packed_ref[0, :, cols] * BF(HD**-0.5), left)
        scores = jnp.where(seen, mm(query, packed_ref[1, :, cols], NT), -1e30)
        most = jnp.max(scores, axis=-1, keepdims=True)
        probs = jnp.exp(scores - most)
        total = jnp.sum(probs, axis=-1, keepdims=True)
        mixed = mm(probs.astype(BF), packed_ref[2, :, cols], NN) / total
        mixed_ref[:, cols] = jnp.where(left, mixed[:ROWS], mixed[ROWS:]).astype(BF)
        logs = most + jnp.log(total)
        totals = jnp.where(lane == 2 * pair, logs[:ROWS], totals)
        totals = jnp.where(lane == 2 * pair + 1, logs[ROWS:], totals)
    total_ref[...] = totals
    values = values + mm(mixed_ref[:, :span], own_out[...], NN)
    for d in range(1, groups):
        mixed = mixed_ref[:, d * span : (d + 1) * span]
        parts = [mm(mixed, far_out[d - 1, j], NN) for j in range(groups)]
        values = values + jnp.concatenate(parts, 1)
    new_ref[...] = values
    for next_ref in next_refs:
        hat, _ = row_stats(values)
        next_ref[...] = (hat * next_norm[0][...] + next_norm[1][...]).astype(BF)


def attend_back_kernel(
    layer, groups, place_ref, grad_ref, x_ref, packed_ref, total_ref, gain_ref, *refs
):
    many = 4 * groups - 2
    targets, sems = refs[-5:-1], refs[-1]
    moved_ref, gain_out, bias_out = refs[many : many + 3]
    new_refs = refs[many + 3 : -5]
    own_qkv, own_out, far_qkv, far_out = targets
    copies = attend_copies(layer, place_ref[0], refs[:many], targets, sems)
    run_at_start(copies)
    grad = grad_ref[...]
    low = grad.astype(BF)
    wait_at_start(copies)
    span = own_qkv.shape[-1]
    grad_mixed = [mm(low, own_out[...], NT).astype(BF)]
    for d in range(1, groups):
        parts = [
            mm(low[:, j * span : (j + 1) * span], far_out[d - 1, j], NT) for j in range(groups)
        ]
        grad_mixed.append(sum(parts).astype(BF))
    grad_mixed = jnp.concatenate(grad_mixed, 1)
    left, seen = pair_masks()
    for pair in range(packed_ref.shape[-1] // (2 * HD)):
        cols = slice(pair * 2 * HD, (pair + 1) * 2 * HD)
        query = stack_pair(packed_ref[0, :, cols] * BF(HD**-0.5), left)
        key = packed_ref[1, :, cols]
        outer = stack_pair(grad_mixed[:, cols], left)
        total = jnp.concatenate(
            [total_ref[:, 2 * pair : 2 * pair + 1], total_ref[:, 2 * pair + 1 : 2 * pair + 2]], 0
        )
        probs = jnp.where(seen, jnp.exp(mm(query, key, NT) - total), 0.0)
        grad_probs = mm(outer, packed_ref[2, :, cols], NT)
        inner = jnp.sum(grad_probs * probs, axis=-1, keepdims=True)
        grad_scores = (probs * (grad_probs - inner)).astype(BF)
        grad_query = mm(grad_scores, key, NN) * HD**-0.5
        moved_ref[0, :, cols] = jnp.where(left, grad_query[:ROWS], grad_query[ROWS:]).astype(BF)
        moved_ref[1, :, cols] = mm(grad_scores, query, TN).astype(BF)
        moved_ref[2, :, cols] = mm(probs.astype(BF), outer, TN).astype(BF)
    back = jnp.zeros_like(grad)
    for s in range(3):
        back = back + mm(moved_ref[s, :, :span], own_qkv[s], NT)
        for d in range(1, groups):
            back = back + mm(moved_ref[s, :, d * span : (d + 1) * span], far_qkv[d - 1, s], NT)
    finish_back(grad, back, x_ref, gain_ref, new_refs, gain_out, bias_out)


def finish_back(grad, back, x_ref, gain_ref, new_refs, gain_out, bias_out):
    hat, scale = row_stats(x_ref[...])
    grad = grad + norm_pull(back, hat, scale, gain_ref[...])
    for new_ref in new_refs:
        new_ref[...] = grad.astype(new_ref.dtype)

    @pl.when(pl.program_id(0) == 0)
    def _():
        gain_out[...] = jnp.zeros_like(gain_out)
        bias_out[...] = jnp.zeros_like(bias_out)

    gain_out[...] += jnp.sum(back * hat, axis=0, keepdims=True)
    bias_out[...] += jnp.sum(back, axis=0, keepdims=True)


def dense_kernel(groups, place_ref, x_ref, gain_ref, bias_ref, *refs):
    many = 8 * groups - 6
    new_ref, normed_ref, act_ref, slope_ref = refs[many : many + 4]
    targets, sems = refs[many + 4 : -1], refs[-1]
    copies = dense_copies(place_ref[0], refs[:many], targets, sems)
    firsts = [targets[0]] + [targets[2].at[d] for d in range(groups - 1)]
    seconds = [targets[1]] + [targets[3].at[d] for d in range(groups - 1)]
    run_at_start(copies)
    values = x_ref[...]
    hat, _ = row_stats(values)
    normed = (hat * gain_ref[...] + bias_ref[...]).astype(BF)
    normed_ref[...] = normed
    wait_at_start(copies)
    span = targets[0].shape[-1]
    chunk = span // 2
    for d in range(groups):
        for part in range(2):
            inner = slice(part * chunk, (part + 1) * chunk)
            cols = slice(d * span + part * chunk, d * span + (part + 1) * chunk)
            act, slope = gelu_both(mm(normed, firsts[d][:, inner], NN))
            act = act.astype(BF)
            act_ref[:, cols] = act
            slope_ref[:, cols] = slope.astype(BF)
            values = values + mm(act, seconds[d][inner], NN)
    new_ref[...] = values


def dense_back_kernel(groups, place_ref, grad_ref, x_ref, slope_ref, gain_ref, *refs):
    many = 8 * groups - 6
    moved_ref, gain_out, bias_out = refs[many : many + 3]
    new_refs = refs[many + 3 : -5]
    targets, sems = refs[-5:-1], refs[-1]
    copies = dense_copies(place_ref[0], refs[:many], targets, sems)
    firsts = [targets[0]] + [targets[2].at[d] for d in range(groups - 1)]
    seconds = [targets[1]] + [targets[3].at[d] for d in range(groups - 1)]
    run_at_start(copies)
    grad = grad_ref[...]
    low = grad.astype(BF)
    wait_at_start(copies)
    span = targets[0].shape[-1]
    chunk = span // 2
    back = jnp.zeros_like(grad)
    for d in range(groups):
        for part in range(2):
            inner = slice(part * chunk, (part + 1) * chunk)
            cols = slice(d * span + part * chunk, d * span + (part + 1) * chunk)
            hidden = mm(low, seconds[d][inner], NT) * slope_ref[:, cols].astype(F32)
            hidden = hidden.astype(BF)
            moved_ref[:, cols] = hidden
            back = back + mm(hidden, firsts[d][:, inner], NT)
    finish_back(grad, back, x_ref, gain_ref, new_refs, gain_out, bias_out)


def image_block(*shape):
    lead = len(shape) - 2
    return pl.BlockSpec(shape, lambda i: (0,) * lead + (i, 0))


def fixed_block(*shape):
    return pl.BlockSpec(shape, lambda i: (0,) * len(shape))


RAW = pl.BlockSpec(memory_space=pl.ANY)


def dense_call(kernel, place, rows, singles, flat, outs, scratch, flops):
    buffers, copies = scratch
    specs = [pl.BlockSpec(memory_space=pltpu.SMEM)]
    specs += [image_block(*r.shape[:-2], ROWS, r.shape[-1]) for r in rows]
    specs += [fixed_block(*r.shape) for r in singles]
    specs += [RAW] * len(flat)
    out_specs = [
        image_block(*o.shape[:-2], ROWS, o.shape[-1]) if o.shape[-2] > 1 else fixed_block(*o.shape)
        for o in outs
    ]
    moved = sum(o.size * o.dtype.itemsize for o in list(outs) + list(rows) + flat)
    return pl.pallas_call(
        kernel,
        grid=(rows[0].shape[-2] // ROWS,),
        in_specs=specs,
        out_specs=out_specs,
        out_shape=outs,
        scratch_shapes=[pltpu.VMEM(b, BF) for b in buffers]
        + [pltpu.SemaphoreType.DMA((copies,))],
        cost_estimate=cost_of(flops, moved),
    )(place, *rows, *singles, *flat)


def cost_of(flops, moved):
    return pl.CostEstimate(
        flops=int(COST * flops), bytes_accessed=int(COST * moved), transcendentals=0
    )


def shape(*dims, kind=BF):
    return jax.ShapeDtypeStruct(dims, kind)


def attend_forward(layer, groups, place, values, gain, bias, weights, follow=()):
    rows, width = values.shape
    outs = (
        shape(rows, width, kind=F32),
        shape(rows, width),
        shape(3, rows, width),
        shape(rows, width),
        shape(rows, 128, kind=F32),
    ) + (shape(rows, width),) * bool(follow)
    return dense_call(
        functools.partial(attend_kernel, layer, groups, bool(follow)),
        place, (values,), (gain, bias) + follow, weights, outs, attend_scratch(width, groups),
        rows * width * (8 * width + 4 * ROWS),
    )


def attend_backward(
    layer, groups, place, grad, values, gain, packed, total, weights, kinds
):
    rows, width = values.shape
    outs = (
        shape(3, rows, width),
        shape(1, width, kind=F32),
        shape(1, width, kind=F32),
    ) + tuple(shape(rows, width, kind=k) for k in kinds)
    return dense_call(
        functools.partial(attend_back_kernel, layer, groups),
        place, (grad, values, packed, total), (gain,), weights, outs,
        attend_scratch(width, groups), rows * width * (8 * width + 10 * ROWS),
    )


def dense_forward(groups, place, values, gain, bias, weights):
    rows, width = values.shape
    hidden = groups * weights[0].shape[-1]
    outs = (
        shape(rows, width, kind=F32),
        shape(rows, width),
        shape(rows, hidden),
        shape(rows, hidden),
    )
    return dense_call(
        functools.partial(dense_kernel, groups),
        place, (values,), (gain, bias), weights, outs, dense_scratch(width, hidden, groups),
        4 * rows * width * hidden,
    )


def dense_backward(groups, place, grad, values, gain, slope, weights):
    rows, width = values.shape
    hidden = groups * weights[0].shape[-1]
    outs = (
        shape(rows, hidden),
        shape(1, width, kind=F32),
        shape(1, width, kind=F32),
        shape(rows, width, kind=F32),
        shape(rows, width),
    )
    return dense_call(
        functools.partial(dense_back_kernel, groups),
        place, (grad, values, slope), (gain,), weights, outs,
        dense_scratch(width, hidden, groups), 4 * rows * width * hidden,
    )


def expert_kernel(rows_ref, *refs):
    weights, (out_ref, act_ref, slope_ref) = refs[:-3], refs[-3:]
    rows = rows_ref[...]
    width = rows.shape[1]
    span = weights[0].shape[1]
    total = jnp.zeros(rows.shape, F32)
    for j, weight in enumerate(weights):
        cols = slice(j * span, (j + 1) * span)
        act, slope = gelu_both(mm(rows, weight[:width], NN))
        act = act.astype(BF)
        act_ref[:, cols] = act
        slope_ref[:, cols] = slope.astype(BF)
        parts = [mm(act, weight[k : k + span], NN) for k in range(width, 2 * width, span)]
        total = total + (jnp.concatenate(parts, 1) if len(parts) > 1 else parts[0])
    out_ref[...] = total.astype(BF)


def expert_back_kernel(grad_ref, slope_ref, *refs):
    weights, (out_ref, hidden_ref) = refs[:-2], refs[-2:]
    grad = grad_ref[...]
    width = grad.shape[1]
    span = weights[0].shape[1]
    total = jnp.zeros(grad.shape, F32)
    for j, weight in enumerate(weights):
        cols = slice(j * span, (j + 1) * span)
        parts = [
            mm(grad[:, k : k + span], weight[width + k : width + k + span], NT)
            for k in range(0, width, span)
        ]
        hidden = (sum(parts) * slope_ref[:, cols].astype(F32)).astype(BF)
        hidden_ref[:, cols] = hidden
        total = total + mm(hidden, weight[:width], NT)
    out_ref[...] = total.astype(BF)


def expert_call(kernel, rows, weights, outs):
    count = rows[0].shape[0]
    tile = 256 if count % 256 == 0 else 128
    hold = [
        pl.BlockSpec(w.shape, lambda i: (0, 0), pipeline_mode=pl.Buffered(1)) for w in weights
    ]
    moved = sum(o.size * o.dtype.itemsize for o in list(outs) + list(rows) + list(weights))
    return pl.pallas_call(
        kernel,
        grid=(count // tile,),
        in_specs=[image_spec(tile, r) for r in rows] + hold,
        out_specs=[image_spec(tile, o) for o in outs],
        out_shape=outs,
        cost_estimate=cost_of(2 * count * sum(w.size for w in weights), moved),
    )(*rows, *weights)


def image_spec(tile, like):
    return pl.BlockSpec((tile, like.shape[1]), lambda i: (i, 0))


def expert_forward(rows, weights):
    count, width = rows.shape
    hidden = len(weights) * weights[0].shape[1]
    outs = (shape(count, width), shape(count, hidden), shape(count, hidden))
    return expert_call(expert_kernel, (rows,), weights, outs)


def expert_backward(grad, slope, weights):
    outs = (shape(*grad.shape), shape(*slope.shape))
    return expert_call(expert_back_kernel, (grad, slope), weights, outs)


def weight_kernel(groups, lines, mover_ref, *refs):
    stats, refs = refs[:lines], refs[lines:]
    count = (len(refs) - 2) // 2
    lefts, rights, (keep_ref, send_ref) = refs[:count], refs[count:-2], refs[-2:]
    half = keep_ref.shape[0]
    turned = [
        left[...] if left.shape[0] == half * 2 else mm(mover_ref[...], left[...], NT).astype(BF)
        for left in lefts
    ]
    at = 0
    columns = keep_ref.shape[1] // groups
    for left, right in zip(turned, rights):
        for s in range(right.shape[0] if len(right.shape) == 3 else 1):
            source = right.at[s] if len(right.shape) == 3 else right
            span = source.shape[1] // groups
            tile = min(source.shape[1], 768)
            for k in range(0, source.shape[1], tile):
                part = mm(left, source[:, k : k + tile], NN).astype(BF)
                for j in range(k, k + tile, min(span, tile)):
                    low = (j // span) * columns + at + j % span
                    high = low + min(span, tile)
                    piece = part[:, j - k : j - k + min(span, tile)]
                    keep_ref[:, low:high] = piece[:half]
                    send_ref[:, low:high] = piece[half:]
            at += span
    if lines:
        rows = [stat[...] for stat in stats]
        room = columns - at
        rows.append(jnp.zeros((room - sum(r.shape[0] for r in rows), half * 2), F32))
        piece = mm(mover_ref[...], jnp.concatenate(rows, 0).astype(BF), NT).astype(BF)
        for d in range(groups):
            keep_ref[:, d * columns + at : (d + 1) * columns] = piece[:half]
            send_ref[:, d * columns + at : (d + 1) * columns] = piece[half:]


def weight_grads(groups, mover, pairs, stats=()):
    width = mover.shape[0]
    columns = sum(r.size // r.shape[-2] for _, r in pairs)
    columns += groups * -(-sum(r.shape[0] for r in stats) // 128) * 128
    out = shape(width // 2, columns)
    rows = pairs[0][1].shape[-2]
    operands = [mover, *stats] + [p[0] for p in pairs] + [p[1] for p in pairs]
    return pl.pallas_call(
        functools.partial(weight_kernel, groups, len(stats)),
        in_specs=[pl.BlockSpec(memory_space=pltpu.VMEM)] * len(operands),
        out_specs=[pl.BlockSpec(memory_space=pltpu.VMEM)] * 2,
        out_shape=(out, out),
        cost_estimate=cost_of(
            2 * width * columns * rows, sum(2 * o.size for o in operands) + 4 * out.size
        ),
    )(*operands)


def dispatch_kernel(part, far, back, extra_ref, lines_ref, gates_ref, rows_ref, *refs):
    seats, got, refs = refs[:far], refs[far : 2 * far], refs[2 * far :]
    out_ref = refs[back]
    tile = out_ref.shape[0]
    base = pl.program_id(0) * tile
    ids = base + lax.broadcasted_iota(jnp.int32, (tile, lines_ref.shape[1]), 0)
    first, second = ids == lines_ref[:1], ids == lines_ref[1:]
    total = mm((first | second).astype(F32).astype(BF), rows_ref[...], NN)
    if back:
        gates = jnp.where(first, gates_ref[:1], 0.0) + jnp.where(second, gates_ref[1:], 0.0)
        refs[2][...] = jnp.sum(total * refs[0][...].astype(F32), axis=1, keepdims=True)
        total = total * jnp.sum(gates, axis=1, keepdims=True)
    else:
        line = base + lax.broadcasted_iota(jnp.int32, (tile, 1), 0)
        total = total + jnp.where(line % part == part - 1, extra_ref[0], 0.0)
    for seat, x in zip(seats, got):
        ids = base + lax.broadcasted_iota(jnp.int32, (tile, seat.shape[1]), 0)
        total = total + mm((ids == seat[...]).astype(F32).astype(BF), x[...], NN)
    out_ref[...] = total.astype(BF)


def dispatch_call(part, slots, extra, lines, gates, rows, seats, got, merged=None):
    tile = 256 if slots % 256 == 0 else 128
    width = rows.shape[1]
    back = merged is not None
    held = [lines, gates, rows, *seats, *got]
    block = pl.BlockSpec((tile, width), lambda i: (i, 0))
    outs = (shape(slots, width),)
    specs = (block,)
    if back:
        outs += (shape(slots, 1, kind=F32),)
        specs += (pl.BlockSpec((tile, 1), lambda i: (i, 0)),)
    inputs = held + [merged] * back
    return pl.pallas_call(
        functools.partial(dispatch_kernel, part, len(got), back),
        grid=(slots // tile,),
        in_specs=[pl.BlockSpec(memory_space=pltpu.SMEM)]
        + [fixed_block(*x.shape) for x in held]
        + [block] * back,
        out_specs=specs,
        out_shape=outs,
        cost_estimate=cost_of(2 * slots * rows.size, 2 * (slots * width + rows.size)),
    )(extra, *inputs)


def picks_of(pack, number, weighted, count):
    ids = lax.broadcasted_iota(jnp.int32, (pack.shape[0], count), 1)
    cols = pack[:, 3 + 2 * number : 5 + 2 * number].astype(jnp.int32)
    first, second = ids == cols[:, :1], ids == cols[:, 1:]
    if not weighted:
        return (first | second).astype(F32).astype(BF)
    return (jnp.where(first, pack[:, :1], 0.0) + jnp.where(second, pack[:, 1:2], 0.0)).astype(BF)


def combine_kernel(pack_ref, x_ref, teacher_ref, *refs):
    rows, (final_ref, grad_ref, low_ref) = refs[:-3], refs[-3:]
    total, pack = x_ref[...], pack_ref[...]
    for number, source in enumerate(rows):
        total = total + mm(picks_of(pack, number, True, source.shape[0]), source[...], NN)
    final_ref[...] = total.astype(BF)
    grad = pack[:, 2:3] * (total - teacher_ref[...].astype(F32))
    grad_ref[...] = grad
    low_ref[...] = grad.astype(BF)


def combine_back_kernel(far, pack_ref, x_ref, grad_ref, logits_ref, *refs):
    rows, refs = refs[: far + 1], refs[far + 1 :]
    router_ref, gain_ref, gain_out, bias_out, *new_refs = refs
    total, pack = mm(logits_ref[...], router_ref[...], NT), pack_ref[...]
    for number, source in enumerate(rows):
        total = total + mm(picks_of(pack, number, False, source.shape[0]), source[...], NN)
    finish_back(grad_ref[...], total, x_ref, gain_ref, new_refs, gain_out, bias_out)


def combine_call(kernel, tiled, held, outs):
    moved = sum(x.size * x.dtype.itemsize for x in list(tiled) + list(held) + list(outs))
    return pl.pallas_call(
        kernel,
        grid=(tiled[0].shape[0] // ROWS,),
        in_specs=[image_block(ROWS, x.shape[1]) for x in tiled]
        + [fixed_block(*x.shape) for x in held],
        out_specs=[
            image_block(ROWS, o.shape[1]) if o.shape[0] > 1 else fixed_block(*o.shape) for o in outs
        ],
        out_shape=outs,
        cost_estimate=cost_of(2 * tiled[0].shape[0] * held[0].size, moved),
    )(*tiled, *held)


def outer_kernel(left_ref, right_ref, *refs):
    part = mm(left_ref[...], right_ref[...], TN)
    for got in refs[:-1]:
        part = part + got[...].astype(F32)
    refs[-1][...] = part.astype(refs[-1].dtype)


def expert_grads(left, right, width, span, first, count, got=None, skip=0, cut_left=True):
    rows = left.shape[0]
    high, low = (span, width) if cut_left else (width, span)
    cut = pl.BlockSpec((rows, span), lambda j: (0, 2 * j + first))
    whole = pl.BlockSpec((rows, width), lambda j: (0, 0))
    more = () if got is None else (got,)
    out = shape(count * high, low)
    return pl.pallas_call(
        outer_kernel,
        grid=(count,),
        in_specs=([cut, whole] if cut_left else [whole, cut])
        + [pl.BlockSpec((high, low), lambda j: (j + skip, 0))] * len(more),
        out_specs=pl.BlockSpec((high, low), lambda j: (j, 0)),
        out_shape=out,
        cost_estimate=cost_of(2 * out.size * rows, 2 * (left.size + right.size + 2 * out.size)),
    )(left, right, *more)


def pinned_all(values, *others):
    return lax.optimization_barrier(tuple(values) + others)[: len(values)]


def pinned(value, *others):
    return lax.optimization_barrier((value,) + others)[0]


def body(
    tokens,
    teacher,
    valid_flags,
    routes,
    capacity,
    norm_gains,
    norm_biases,
    attn_qkv,
    attn_out,
    mlp_in,
    mlp_out,
    router,
    expert_in,
    expert_out,
):
    owners = lax.axis_size("expert")
    groups = lax.axis_size("tensor")
    place = lax.axis_index("expert")
    group = lax.axis_index("tensor")
    local_rows, width = tokens.shape
    experts = router.shape[1]
    image_count = local_rows // SEQ
    images = -(-image_count // groups)
    own_rows = images * ROWS
    all_rows = groups * own_rows
    capacity_most = 4 * (3 * local_rows // (4 * experts))
    used = -(-capacity_most // (2 * groups))
    part = -(-(used + 1) // 16) * 16
    slots = owners * part
    gains = norm_gains.astype(F32)
    biases = norm_biases.astype(F32)

    def relative(rows, fill, count):
        shape = rows.shape[1:]
        grid = rows.reshape((image_count, SEQ) + shape)
        grid = jnp.pad(
            grid,
            [(0, groups * images - image_count), (0, ROWS - SEQ)] + [(0, 0)] * len(shape),
            constant_values=fill,
        )
        taken = [
            lax.dynamic_slice_in_dim(grid, (group ^ d) * images, images, 0) for d in range(count)
        ]
        return jnp.concatenate(taken, 0).reshape((count * own_rows,) + shape)

    def absolute(rows):
        shape = rows.shape[1:]
        grid = rows.reshape((groups * images, ROWS) + shape)
        taken = [
            lax.dynamic_slice_in_dim(grid, (group ^ d) * images, images, 0) for d in range(groups)
        ]
        grid = jnp.concatenate(taken, 0)[:image_count, :SEQ]
        return grid.reshape((local_rows,) + shape)

    place_ref = jnp.full((1,), place, jnp.int32)
    gain_rows = [gains[j : j + 1] for j in range(4)]
    bias_rows = [biases[j : j + 1] for j in range(4)]

    quarter = place % 4

    def attend_piece(layer):
        span = attn_out.shape[1]
        rows, few = width // 4, span // 4
        qkv_part = lax.dynamic_slice(
            attn_qkv, (layer, 0, quarter * rows, 0), (1, 3, rows, span)
        ).reshape(3 * rows, span)
        out_part = lax.dynamic_slice(attn_out, (layer, quarter * few, 0), (1, few, width))[0]
        parts = [out_part[:, j * span : (j + 1) * span] for j in range(groups)]
        return jnp.concatenate([qkv_part] + parts, 0)

    def rows_of(weight, number):
        rows = weight.shape[0] // 4
        return lax.dynamic_slice_in_dim(weight, number * rows, rows, 0)

    def over_tensor(value):
        return [swap(value, "tensor", d) for d in range(1, groups)]

    def both_cores(value):
        return [value, swap(value, "expert", 1)]

    last = [None]

    def after(*values):
        if last[0] is not None:
            values = pinned_all(values, last[0])
        return values if len(values) > 1 else values[0]

    def mark(value):
        last[0] = value
        return value

    def leg(parts, distance):
        return [swap(part, "expert", distance) for part in parts]

    def joined(first, second, third, last):
        return [x for four in zip(first, third, second, last) for x in four]

    piece_first = mark(attend_piece(0))
    first_x = over_tensor(piece_first)
    piece_in = mark(rows_of(after(mlp_in), quarter))
    piece_out = mark(rows_of(after(mlp_out), place % 2 + place // 4 % 2 * 2))
    piece_second = mark(attend_piece(1))
    tokens = after(tokens)
    start = mark(relative(tokens, 0, 1).astype(F32))
    first_x = [after(x) for x in first_x]
    in_x, out_x = over_tensor(piece_in), over_tensor(piece_out)
    second_x = over_tensor(piece_second)
    first_y, first_c = leg(first_x, 2), leg(first_x, 1)
    first_l = leg(first_y, 1)
    weights_first = [attn_qkv, attn_out] + joined(first_x, first_y, first_c, first_l)

    room = 2 * used
    kind = jnp.int32
    routes = pinned(routes, first_x[0])
    expert_of = jnp.concatenate([routes[:, 0], routes[:, 1]])
    owner = jnp.tile(jnp.arange(local_rows, dtype=kind) // (SEQ * images), 2)
    of_expert = (expert_of[:, None] == jnp.arange(experts, dtype=kind)).astype(kind)
    of_owner = (owner[:, None] == jnp.arange(groups, dtype=kind)).astype(kind)
    both = (
        (expert_of * groups + owner)[:, None] == jnp.arange(experts * groups, dtype=kind)
    ).astype(kind)
    earlier = (jnp.cumsum(both, axis=0) - both).reshape(-1, experts, groups)
    ahead = jnp.sum(earlier * of_expert[:, :, None], axis=1)
    rank = jnp.sum(ahead * of_owner, axis=1)
    kept_mask = jnp.sum(ahead, axis=1) < jnp.sum(of_expert * capacity[None, :], axis=1)
    held = jnp.sum(both * kept_mask[:, None].astype(kind), axis=0).reshape(experts, groups)
    inside = jnp.minimum(held, room)
    beyond = held - inside
    free = room - inside

    def before(counts):
        return jnp.cumsum(counts, axis=1) - counts

    def of_pair(table):
        return jnp.sum(of_expert[:, :, None] * table[None], axis=1)

    late = jnp.sum(of_pair(before(beyond)) * of_owner, axis=1) + rank - room
    free_from = of_pair(before(free))
    hit = (late[:, None] >= free_from) & (late[:, None] < free_from + of_pair(free))
    hit = hit.astype(kind)
    fits = rank < room
    at = jnp.where(fits, rank, jnp.sum(hit * (of_pair(inside) + late[:, None] - free_from), axis=1))
    home = jnp.where(fits, owner, jnp.sum(hit * jnp.arange(groups, dtype=kind), axis=1))
    row_of = (2 * expert_of + at // used) * part + at % used

    def own_pairs(values):
        return relative(values.reshape(2, local_rows).T, -1, 1)

    local_row = own_pairs(jnp.where(kept_mask & (owner == group) & (home == group), row_of, -1))
    most = min(experts, 2 * SEQ * images // capacity_most)
    rest = min(2 * SEQ * images - most * capacity_most, capacity_most) - room
    most = most * (capacity_most - room) + max(rest, 0)
    most = -(-most // 16) * 16
    few = min(64, most)
    masks = []
    for d in range(1, groups):
        masks.append(kept_mask & (owner == group) & (home == group ^ d))
        masks.append(kept_mask & (owner == group ^ d) & (home == group))
    masks = jnp.stack(masks, 1).astype(kind)
    ranks = jnp.cumsum(masks, axis=0) - masks
    ranks = jnp.where(masks > 0, ranks, -1)
    guest_out, guest_in = [], []
    for d in range(1, groups):
        guest_out.append(own_pairs(ranks[:, 2 * d - 2]))
        named = ranks[:, 2 * d - 1][None, :] == jnp.arange(most, dtype=kind)[:, None]
        guest_in.append(jnp.sum(jnp.where(named, row_of[None, :] + 1, 0), axis=1) - 1)
    distances = [1 << k for k in range(owners.bit_length() - 1)]

    def wider(value, step, *others):
        got = swap(value, "expert", step)
        return jnp.maximum(value, pinned(got, *others) if others else got)

    crowd = wider(jnp.full((8, 128), jnp.max(beyond.sum(0)), kind), 1)
    routes_own = relative(routes, 0, 1)
    valid_rows = relative(jnp.repeat(valid_flags.astype(F32), SEQ)[:, None], 0, 1)

    in_x = pinned_all(in_x, *first_l)
    start = pinned(start, *in_x, local_row, crowd)
    after_attn, normed_first, packed_first, mixed_first, total_first = attend_forward(
        0, groups, place_ref, start, gain_rows[0], bias_rows[0], weights_first
    )
    crowd = wider(crowd, 4, after_attn)
    out_x = pinned_all(out_x, after_attn)
    second_x = pinned_all(second_x, *out_x)
    in_y, in_c = leg(in_x, 2), leg(in_x, 1)
    out_y, out_c = leg(out_x, 4), leg(out_x, 1)
    in_y, out_y = pinned_all(in_y, after_attn), pinned_all(out_y, *second_x)
    crowd = wider(crowd, 8, *out_y)
    weights_dense = [mlp_in, mlp_out] + joined(in_x, in_y, in_c, leg(in_y, 1))
    weights_dense += joined(out_x, out_y, out_c, leg(out_y, 1))
    second_y, second_c = leg(second_x, 2), leg(second_x, 1)
    after_dense, normed_dense, dense_act, dense_slope = dense_forward(
        groups, place_ref, pinned(after_attn, crowd, *second_x), gain_rows[1], bias_rows[1],
        weights_dense,
    )
    second_y = pinned_all(second_y, after_dense)
    weights_second = [attn_qkv, attn_out] + joined(second_x, second_y, second_c, leg(second_y, 1))
    second = attend_forward(
        1, groups, place_ref, pinned(after_dense, crowd), gain_rows[2], bias_rows[2],
        weights_second, (gain_rows[3], bias_rows[3]),
    )
    after_second, normed_second, packed_second, mixed_second, total_second, normed_expert = second
    for step in [2] + distances[4:]:
        crowd = wider(crowd, step, after_second)
    logits = mm(normed_expert, router, NN)
    picker = routes_own[:, :, None] == jnp.arange(experts, dtype=kind)[None, None, :]
    chosen = jnp.sum(jnp.where(picker, logits[:, None, :], 0.0), axis=2)
    gate_vals = jax.nn.softmax(chosen, axis=1)
    gate_lines = gate_vals.T
    local_lines = local_row.T
    slot_ids = jnp.arange(slots, dtype=kind)

    def guests(count):
        ids = jnp.arange(count, dtype=kind)[:, None]
        return [(ids == g[None, :, 0], ids == g[None, :, 1]) for g in guest_out]

    def chosen_rows(count, rows):
        return [mm((a | b).astype(BF), rows, NN) for a, b in guests(count)]

    def returned_rows(count, rows):
        return [
            mm((g[:count, None] == slot_ids[None, :]).astype(BF), rows, NN).astype(BF)
            for g in guest_in
        ]

    def seats(count):
        return [g[None, :count] for g in guest_in]

    def over(rows):
        return [swap(x, "tensor", d + 1) for d, x in enumerate(rows)]

    def sized(branch, *operands):
        if few == most:
            return branch(few)(*operands)
        return lax.cond(crowd[0, 0] <= few, branch(few), branch(most), *operands)

    def grown(rows):
        return jnp.pad(rows, ((0, most - rows.shape[0]), (0, 0)))

    def across(rows):
        return lax.all_to_all(
            rows.reshape(owners, part, width), "expert", split_axis=0, concat_axis=0, tiled=True
        ).reshape(slots, width)

    images_valid = jnp.sum(valid_flags.astype(F32)).reshape(1)
    blank = jnp.zeros((2, own_rows), F32)

    def dispatch(count):
        def branch(rows):
            got = over([x.astype(BF) for x in chosen_rows(count, rows)])
            return dispatch_call(
                part, slots, images_valid, local_lines, blank, rows, seats(count), got
            )[0]

        return branch

    sent_rows = sized(dispatch, normed_expert)
    span = expert_in.shape[2]
    blocks = [expert_out[0, :, k : k + span] for k in range(0, width, span)]
    expert_own = pinned(jnp.concatenate([expert_in[0]] + blocks, 0), sent_rows)
    expert_parts = [x for w in [expert_own] + over_tensor(expert_own) for x in both_cores(w)]
    rows_in = across(sent_rows)
    valid_count = SEQ * jnp.sum(rows_in[part - 1 :: part, :1].astype(F32))
    teacher_rel = relative(teacher, 0, 1)
    scale = (local_rows * owners / valid_count) * valid_rows
    rows_in = pinned(rows_in, teacher_rel, scale)
    expert_rows, act, slope = expert_forward(rows_in, expert_parts)
    block = width // owners
    feature = jnp.arange(width, dtype=jnp.int32)

    def mover_of(distances):
        ahead, turned = feature // block, 0
        for distance in reversed(distances):
            turned = turned + distance * (ahead % 2)
            ahead = ahead // 2
        source = (turned ^ place) * block + feature % block
        return (source[:, None] == feature[None, :]).astype(BF)

    mover = mover_of(distances)
    turned_order = [1, 4, 2] + distances[3:]
    mover_turned = mover_of(turned_order)

    pairs = [x.astype(F32) for x in (local_row, *guest_out)]
    pack = jnp.concatenate([gate_vals, scale] + pairs, 1)
    pack = jnp.pad(pack, ((0, 0), (0, 128 - pack.shape[1])))
    merged = across(expert_rows)
    turned_rows = [
        mm(m, pinned(rows, expert_rows), NT).astype(BF)
        for m, rows in (
            (mover, normed_second), (mover_turned, normed_dense), (mover, normed_first)
        )
    ]
    merged, pack, *turned_rows = pinned_all((merged, pack, *turned_rows), expert_rows)

    outs = (shape(own_rows, width), shape(own_rows, width, kind=F32), shape(own_rows, width))

    def combine(count):
        def branch(rows):
            got = over(returned_rows(count, rows))
            results = combine_call(
                combine_kernel, (pack, after_second, teacher_rel), (rows, *got), outs
            )
            return tuple(results) + tuple(grown(x) for x in got)

        return branch

    final_low, grad_final, grad_low, *lodged = sized(combine, merged)

    def dispatch_back(count):
        def branch(rows, merged, *lodged):
            sent, parts = [], []
            for (a, b), x, taken in zip(guests(count), lodged, chosen_rows(count, rows)):
                gates = jnp.sum(
                    jnp.where(a, gate_lines[:1], 0.0) + jnp.where(b, gate_lines[1:], 0.0),
                    axis=1,
                    keepdims=True,
                )
                sent.append((gates * taken).astype(BF))
                inner = jnp.sum(taken * x[:count].astype(F32), axis=1, keepdims=True)
                parts.append(grown(inner))
            results = dispatch_call(
                part, slots, images_valid, local_lines, gate_lines, rows, seats(count),
                over(sent), merged,
            )
            return tuple(results) + tuple(parts)

        return branch

    sent_back, grad_slot_gate, *grad_guest_gate = sized(
        dispatch_back, grad_low, merged, *lodged
    )
    final_far = over_tensor(pinned(final_low, sent_back))
    grad_out_rows = across(sent_back)
    grad_rows, grad_hidden = expert_backward(
        pinned(grad_out_rows, *final_far), slope, expert_parts
    )
    grad_back = across(grad_rows)

    def start_groups(total):
        span = total.shape[1] // groups
        sent = [total[:, d * span : (d + 1) * span].astype(BF) for d in range(1, groups)]
        return total[:, :span], sent

    def start_rows(total):
        rows = total.shape[0] // 2
        return total[:rows], [total[rows:].astype(BF)]

    def cross(sent):
        return [swap(x, "tensor", d + 1) for d, x in enumerate(sent)]

    def along(sent, distance):
        return [swap(x, "expert", distance) for x in sent]

    def finish(keep, got, *after):
        total = keep.astype(F32)
        for x in got:
            total = total + (pinned(x, *after) if after else x).astype(F32)
        return total

    act, rows_in, grad_slot_gate = pinned_all((act, rows_in, grad_slot_gate), grad_rows)
    grad_own = []
    for choice in range(2):
        taken = slot_ids[:, None] == local_row[None, :, choice]
        total = jnp.sum(jnp.where(taken, grad_slot_gate, 0.0), axis=0)
        for pair, values in zip(guests(most), grad_guest_gate):
            total = total + jnp.sum(jnp.where(pair[choice], values, 0.0), axis=0)
        grad_own.append(total)
    grad_own = jnp.stack(grad_own, 1)
    span = expert_in.shape[2]
    def both_shares(left, right, got, cut_left):
        others = groups - 1
        sent = mark(
            expert_grads(after(left), right, width, span, 2, others, after(got), 1, cut_left)
        )
        keep = mark(expert_grads(after(left), right, width, span, 0, 1, got, 0, cut_left))
        rows = sent.shape[0] // others
        return keep, [sent[d * rows : (d + 1) * rows] for d in range(others)]

    sent = mark(expert_grads(act, grad_out_rows, width, span, 1, groups))
    got_eo = along([sent], 1)[0]
    own_gates = gate_vals
    grad_chosen = own_gates * (grad_own - jnp.sum(own_gates * grad_own, axis=1, keepdims=True))
    grad_logits = jnp.sum(
        jnp.where(picker, grad_chosen[:, :, None], 0.0), axis=1
    ).astype(BF)
    grad_router = mm(grad_logits, normed_expert, TN)
    sent = mark(
        expert_grads(after(rows_in), grad_hidden, width, span, 1, groups, None, 0, False)
    )
    got_ei = along([sent], 1)[0]
    keep_eo, sent_eo = both_shares(act, grad_out_rows, got_eo, True)
    got_eo = cross(sent_eo)
    activations = absolute(jnp.concatenate([final_low] + list(pinned_all(final_far, keep_eo)), 0))
    mark(activations)
    keep_ei, sent_ei = both_shares(rows_in, grad_hidden, got_ei, False)
    grad_back = pinned(grad_back, *sent_ei, keep_ei, *got_eo, activations, grad_router)

    outs = (shape(1, width, kind=F32),) * 2 + (
        shape(own_rows, width, kind=F32), shape(own_rows, width),
    )

    def combine_back(count):
        def branch(rows):
            results = combine_call(
                functools.partial(combine_back_kernel, groups - 1),
                (pack, after_second, grad_final, grad_logits),
                (rows, *over(returned_rows(count, rows)), router, gain_rows[3]),
                outs,
            )
            return tuple(results)

        return branch

    gain_four, bias_four, grad_second, low_second = sized(combine_back, grad_back)
    got_ei = cross([pinned(p, grad_second) for p in sent_ei])

    mark(grad_second)
    def arrive(keep, got):
        return finish(keep, [after(x) for x in got])

    grads_second, gain_three, bias_three, grad_dense, low_dense = attend_backward(
        1, groups, place_ref, grad_second, after_dense, gain_rows[2], packed_second,
        total_second, weights_second, (F32, BF),
    )
    mark(grad_dense)
    got_ei = [after(x) for x in got_ei]
    keep_a, send_a = weight_grads(
        groups,
        mover,
        [(pinned(turned_rows[0], *got_ei), grads_second), (low_second, mixed_second)],
    )
    mark(send_a)
    got_a = along([send_a], 1)
    low_dense = after(low_dense)
    keep_b, send_b = weight_grads(groups, mover, [(low_dense, dense_act)])
    mark(send_b)
    got_b = along([send_b], 1)
    keep_a, sent_a = start_groups(arrive(keep_a, got_a).astype(BF))
    mark(sent_a[0])
    got_a = cross(sent_a)
    grad_hidden, gain_two, bias_two, grad_attn, low_first = dense_backward(
        groups, place_ref, after(grad_dense), after_attn, gain_rows[1], dense_slope, weights_dense,
    )
    mark(grad_attn)
    keep_b, sent_b = start_rows(arrive(keep_b, got_b).astype(BF))
    mark(sent_b[0])
    got_b = along(sent_b, 2)

    got_a = [after(x) for x in got_a]
    stats = [gain_two, gain_three, gain_four, bias_two, bias_three, bias_four]
    keep_c, send_c = weight_grads(
        groups,
        mover_turned,
        [
            (pinned(turned_rows[1], *got_a), grad_hidden),
            (low_first, mixed_first),
        ],
        stats + [grad_router],
    )
    mark(send_c)
    got_c = along([send_c], 1)
    keep_a, sent_a = start_rows(arrive(keep_a, got_a).astype(BF))
    mark(sent_a[0])
    got_a = along(sent_a, 2)
    keep_c, sent_c = start_rows(arrive(keep_c, got_c).astype(BF))
    mark(sent_c[0])
    got_c = along(sent_c, 4)
    grads_first, gain_one, bias_one, grad_start = attend_backward(
        0, groups, place_ref, after(grad_attn), start, gain_rows[0], packed_first, total_first,
        weights_first, (BF,),
    )
    mark(grad_start)
    start_far = over_tensor(grad_start)
    got_b = [after(x) for x in got_b]
    keep_d, send_d = weight_grads(
        groups,
        mover,
        [(pinned(turned_rows[2], *got_b), grads_first)],
        [gain_one, bias_one],
    )
    mark(send_d)
    got_d = along([send_d], 1)
    keep_b, sent_b = start_groups(arrive(keep_b, got_b).astype(BF))
    mark(sent_b[0])
    got_b = cross(sent_b)
    keep_a, sent_a = start_rows(arrive(keep_a, got_a))
    mark(sent_a[0])
    got_a = along(sent_a, 4)
    total_c = mark(arrive(keep_c, got_c).astype(BF))
    total_d = arrive(keep_d, got_d).astype(BF)
    span = total_d.shape[1] // groups
    cut = attn_out.shape[1]
    far_d = [
        jnp.concatenate([total_d[:, d * span : d * span + cut] for d in range(groups)], 1),
        jnp.concatenate([total_d[:, d * span + cut : (d + 1) * span] for d in range(groups)], 1),
    ]
    keep_d, sent_d = start_groups(far_d[0])
    keep_e, sent_e = start_rows(far_d[1])
    mark(sent_e[0])
    got_d = cross(sent_d)
    got_e = along(sent_e, 2)
    keep_c, sent_c = start_rows(after(total_c))
    mark(sent_c[0])
    got_c = along(sent_c, 2)
    start_far = [after(x) for x in start_far]
    input_grad = mark(absolute(jnp.concatenate([grad_start] + start_far, 0)))
    keep_a, sent_a = start_rows(arrive(keep_a, got_a))
    mark(sent_a[0])
    got_a = along(sent_a, 8)
    keep_b, sent_b = start_rows(arrive(keep_b, got_b))
    mark(sent_b[0])
    got_b = along(sent_b, 4)
    keep_d, sent_d = start_rows(arrive(keep_d, got_d))
    mark(sent_d[0])
    got_d = along(sent_d, 2)
    keep_e, sent_e = start_groups(arrive(keep_e, got_e))
    mark(sent_e[0])
    got_e = cross(sent_e)
    keep_c, sent_c = start_groups(arrive(keep_c, got_c))
    mark(sent_c[0])
    got_c = cross(sent_c)
    total_a = mark(arrive(keep_a, got_a))
    keep_b, sent_b = start_rows(arrive(keep_b, got_b))
    mark(sent_b[0])
    got_b = along(sent_b, 8)
    total_d = arrive(keep_d, got_d)
    total_e = arrive(keep_e, got_e)
    keep_d, sent_d = start_rows(jnp.concatenate([total_d, total_e], 1))
    mark(sent_d[0])
    got_d = along(sent_d, 4)
    keep_c, sent_c = start_rows(arrive(keep_c, got_c))
    mark(sent_c[0])
    got_c = along(sent_c, 8)
    total_b = mark(arrive(keep_b, got_b))
    keep_d, sent_d = start_rows(arrive(keep_d, got_d))
    mark(sent_d[0])
    got_d = along(sent_d, 8)
    keep_eo, keep_ei = pinned_all((keep_eo, keep_ei), sent_d[0])
    grad_expert_out, grad_expert_in = finish(keep_eo, got_eo), finish(keep_ei, got_ei)
    total_c = arrive(keep_c, got_c)
    total_d = arrive(keep_d, [pinned(x, grad_expert_out, grad_expert_in, total_c) for x in got_d])
    joint = jnp.concatenate([total_a, total_b, total_c, total_d], 1)
    step = 16
    while step < owners:
        keep, sent = start_rows(joint)
        joint = finish(keep, along(sent, step))
        step *= 2
    spans = [attn_out.shape[1], mlp_in.shape[1], -(-(6 + experts) // 128) * 128]
    widths = [4 * spans[0], spans[1], spans[1], spans[0], spans[2], 3 * spans[0], 128]
    taken, at = [], 0
    for span in widths:
        taken.append(joint[:, at : at + span])
        at += span
    two, grad_mlp_out, grad_mlp_in = taken[0], taken[1].T, taken[2]
    one = jnp.concatenate([taken[5], taken[3]], 1)
    lines, last_lines = taken[4], taken[6]
    joint_small = jnp.concatenate(
        [last_lines[:, :1], lines[:, :3], last_lines[:, 1:2], lines[:, 3 : 6 + experts]], 1
    )

    def split_attention(total):
        span = total.shape[1] // 4
        return jnp.stack([total[:, s * span : (s + 1) * span] for s in range(3)]), total[:, -span:].T

    qkv_one, out_one = split_attention(one)
    qkv_two, out_two = split_attention(two)
    small = joint_small.T
    return (
        activations,
        input_grad,
        small[:4],
        small[4:7],
        small[7],
        jnp.stack([qkv_one, qkv_two]),
        jnp.stack([out_one, out_two]),
        grad_mlp_in,
        grad_mlp_out,
        small[8:].T,
        grad_expert_in[None],
        grad_expert_out[None],
    )


def solution(mesh):
    in_specs = (
        P("expert", None),
        P("expert", None),
        P("expert"),
        P("expert", None),
        P(),
        P(),
        P(),
        P(None, None, None, "tensor"),
        P(None, "tensor", None),
        P(None, "tensor"),
        P("tensor", None),
        P(),
        P("expert", None, "tensor"),
        P("expert", "tensor", None),
    )
    out_specs = (
        P("expert", None),
        P("expert", None),
        P(None, "expert"),
        P(None, "expert"),
        P("expert"),
        P(None, None, "expert", "tensor"),
        P(None, "tensor", "expert"),
        P("expert", "tensor"),
        P("tensor", "expert"),
        P("expert", None),
        P("expert", None, "tensor"),
        P("expert", "tensor", None),
    )
    return jax.shard_map(body, mesh=mesh, in_specs=in_specs, out_specs=out_specs, check_vma=False)
```
